512 devices in a mesh: group: 16 (over x, y), dev: 32 (over z, core).
Axes of the slice: x: 4, y: 4, z: 16, core: 2. Of those that a mesh axis runs over, the one named last changes fastest.
Arguments:
- embeddings: bfloat16 [655360, 768], P(('group', 'dev')), may hold values from -6 to 6
- projection: bfloat16 [256, 768], replicated, may hold values from -0.21875 to 0.21875
- triplets: int32 [3, 1048576], P(None, ('group', 'dev')), may hold values from 0 to 3327, as said below
- cotangent: float32 [1048576], P(('group', 'dev')), may hold values from -24 to 24
- wanted_rows: int32 [8192, 128], P(('group', 'dev')), may hold values from -1 to 1279, as said below
Outputs:
- row_grad: bfloat16 [655360, 768], P(('group', 'dev'))
- weight_grad: float32 [256, 768], replicated
The draws below stay inside these ranges and needn't reach their ends.
Inputs may be any that keep to these rules, and one draw needn't show every extreme that they name: `wanted_rows`: in each list the live entries come first and are distinct rows of the owning device, the rest are -1; each list holds from 128 // 4 (at least 1) to 128 live entries; all lists of some group of requesters are full, and all lists sent to some group are full. `triplets`: anchors are below 1280; a positive or negative below 1280 is one of the device's own rows, else 1280 + h * 128 + s names a live slot s of the device's list for group h.
All inputs are finite; a program needn't handle non-finite values.
Results may differ from the reference program's by a relative error of at most 0.0058.
Values may be sent and summed in bfloat16 or wider, within the bound.
No kernel may reach another device: no remote copies, remote signals or barrier semaphores. Data moves between devices by JAX's collectives and lax.ppermute only.
A program may use at most 64 MiB of HBM per device.

```python
import math
import jax
import jax.numpy as jnp
from jax import lax

D = 768
K = 256
ROWS_DEV = 1280
TRIP = 2048
SLOTS = 128
GROUPS = 16
MEMBERS = 32
ROWS = 655360
TRIPLETS = 1048576


def pair_counts(key):
    total_devices = GROUPS * MEMBERS
    subkeys = jax.random.split(jax.random.fold_in(key, 11), 3)
    lowest = max(1, SLOTS // 4)
    counts = jax.random.randint(subkeys[0], (total_devices, GROUPS), lowest, SLOTS + 1)
    full_group = jax.random.randint(subkeys[1], (), 0, GROUPS)
    full_owner = jax.random.randint(subkeys[2], (), 0, GROUPS)
    device_group = jnp.arange(total_devices) // MEMBERS
    counts = jnp.where(device_group[:, None] == full_group, SLOTS, counts)
    counts = jnp.where(jnp.arange(GROUPS)[None, :] == full_owner, SLOTS, counts)
    return counts.astype(jnp.int32)


def draw_wanted_rows(key, part):
    counts = pair_counts(key)
    total_devices = GROUPS * MEMBERS
    subkeys = jax.random.split(jax.random.fold_in(key, 12), total_devices * GROUPS)
    orders = jax.vmap(lambda one_key: jax.random.permutation(one_key, ROWS_DEV))(subkeys)
    first_order = orders[0]
    first_order = jnp.where(first_order == ROWS_DEV - 1, first_order[0], first_order)
    first_order = first_order.at[0].set(ROWS_DEV - 1)
    orders = orders.at[0].set(first_order)
    chosen = orders[:, :SLOTS].reshape(total_devices, GROUPS, SLOTS)
    places = jnp.arange(SLOTS)
    listed = jnp.where(places[None, None, :] < counts[:, :, None], chosen, -1)
    return listed.reshape(total_devices * GROUPS, SLOTS).astype(jnp.int32)


def pick_rows(subkeys, counts, total_devices):
    shape = (total_devices, TRIP)
    own_choice = jax.random.randint(subkeys[0], shape, 0, ROWS_DEV)
    peer = jax.random.randint(subkeys[1], shape, 0, GROUPS)
    live = jnp.take_along_axis(counts, peer, axis=1)
    offset = jax.random.randint(subkeys[2], shape, 0, 1 << 20) % live
    remote = ROWS_DEV + peer * SLOTS + offset
    usage = jax.random.randint(subkeys[3], shape, 0, 4)
    return jnp.where(usage == 0, own_choice, remote)


def draw_triplets(key, part):
    counts = pair_counts(key)
    total_devices = GROUPS * MEMBERS
    subkeys = jax.random.split(jax.random.fold_in(key, 13), 9)
    anchors = jax.random.randint(subkeys[0], (total_devices, TRIP), 0, ROWS_DEV)
    positives = pick_rows(subkeys[1:5], counts, total_devices)
    negatives = pick_rows(subkeys[5:9], counts, total_devices)
    highest = ROWS_DEV + (GROUPS - 1) * SLOTS + counts[:, GROUPS - 1] - 1
    positives = positives.at[:, 0].set(highest)
    negatives = negatives.at[:, 0].set(ROWS_DEV - 1)
    stacked = jnp.stack([anchors, positives, negatives], axis=0)
    return stacked.reshape(3, total_devices * TRIP).astype(jnp.int32)


def block_scale(key, extent, cuts, least, largest):
    def one(position, blocks):
        steps = jax.random.uniform(jax.random.fold_in(jax.random.fold_in(key, 6), position), (blocks,), jnp.float32, least / len(cuts), largest / len(cuts))
        return jnp.repeat(jnp.exp(steps), extent[position] // blocks).reshape((-1,) + (1,) * (len(extent) - position - 1))

    level = one(*cuts[0])
    for cut in cuts[1:]:
        level = level * one(*cut)
    return level


def scatter_about(rng, dims, width, reach, cuts=(), kind=jnp.bfloat16):
    values = width * jax.random.normal(rng, dims, jnp.float32)
    if cuts:
        values = values * block_scale(rng, dims, cuts, -0.22, 0.18)
    return jnp.clip(values, -reach, reach).astype(kind)


def setup_inputs(seed: int = 0) -> dict:
    streams_of = jax.random.split(jax.random.key(seed), 6)
    embeddings = scatter_about(streams_of[0], (ROWS, D), 1.0, 6.0, ((0, 512),))
    projection = scatter_about(streams_of[1], (K, D), D ** -0.5, 0.21875)
    triplets = draw_triplets(jax.random.fold_in(streams_of[5], 71), 0)
    cotangent = scatter_about(streams_of[3], (TRIPLETS,), 4.0, 24.0, ((0, 512),), jnp.float32)
    wanted_rows = draw_wanted_rows(jax.random.fold_in(streams_of[5], 71), 0)
    return {"embeddings": embeddings, "projection": projection, "triplets": triplets, "cotangent": cotangent, "wanted_rows": wanted_rows}


distance_scale = 0.0625
margin = 1.0
pull_share = 0.5

def triplet_gradients(lookup, triple, cotangent):
    anchor_rows = lookup[triple[0]].astype(jnp.float32)
    positive_rows = lookup[triple[1]].astype(jnp.float32)
    negative_rows = lookup[triple[2]].astype(jnp.float32)
    to_positive = anchor_rows - positive_rows
    to_negative = anchor_rows - negative_rows
    near = distance_scale * lax.optimization_barrier(jnp.sum(to_positive * to_positive, axis=1))
    far = distance_scale * lax.optimization_barrier(jnp.sum(to_negative * to_negative, axis=1))
    hinge_gate = jax.nn.sigmoid(margin + near - far)
    pull_factor = 2.0 * distance_scale * cotangent * (1.0 - pull_share + pull_share * hinge_gate)
    push_factor = 2.0 * distance_scale * cotangent * pull_share * hinge_gate
    pull_term = pull_factor[:, None] * to_positive
    push_term = push_factor[:, None] * to_negative
    gradient = jnp.zeros(lookup.shape, jnp.float32)
    gradient = gradient.at[triple[0]].add(pull_term - push_term)
    gradient = gradient.at[triple[1]].add(-pull_term)
    gradient = gradient.at[triple[2]].add(push_term)
    return gradient

def reference(embeddings, projection, triplets, cotangent, wanted_rows):
    contract = (((1,), (1,)), ((), ()))
    projected = lax.dot_general(embeddings, projection, contract, preferred_element_type=jnp.float32).astype(jnp.bfloat16)
    total_devices = GROUPS * MEMBERS
    group_index = jnp.arange(GROUPS, dtype=jnp.int32)

    def accumulate(device, summed):
        member = device % MEMBERS
        first_row = (device * ROWS_DEV).astype(jnp.int32)
        wanted = lax.dynamic_slice_in_dim(wanted_rows, (device * GROUPS).astype(jnp.int32), GROUPS, 0)
        owners = ((group_index * MEMBERS + member) * ROWS_DEV)[:, None] + jnp.maximum(wanted, 0)
        owners = owners.reshape(-1).astype(jnp.int32)
        own_rows = lax.dynamic_slice_in_dim(projected, first_row, ROWS_DEV, 0)
        lookup = jnp.concatenate([own_rows, projected[owners]], axis=0)
        triple = lax.dynamic_slice_in_dim(triplets, (device * TRIP).astype(jnp.int32), TRIP, 1)
        weights_here = lax.dynamic_slice_in_dim(cotangent, (device * TRIP).astype(jnp.int32), TRIP, 0)
        gradient = triplet_gradients(lookup, triple, weights_here)
        current = lax.dynamic_slice_in_dim(summed, first_row, ROWS_DEV, 0)
        summed = lax.dynamic_update_slice_in_dim(summed, current + gradient[:ROWS_DEV], first_row, 0)
        remote_grad = lax.optimization_barrier(gradient[ROWS_DEV:].astype(jnp.bfloat16))
        return summed.at[owners].add(remote_grad.astype(jnp.float32))
    row_total = lax.fori_loop(0, total_devices, accumulate, jnp.zeros((ROWS, K), jnp.float32))
    row_rounded = row_total.astype(jnp.bfloat16)
    row_grad = jnp.dot(row_rounded, projection, preferred_element_type=jnp.float32).astype(jnp.bfloat16)
    weight_total = lax.dot_general(row_rounded, embeddings, (((0,), (0,)), ((), ())), preferred_element_type=jnp.float32)
    weight_grad = weight_total * (1.0 / math.sqrt(TRIPLETS))
    return (row_grad, weight_grad)
```

```python
import functools
import math

import jax
import jax.numpy as jnp
from jax import lax
from jax.experimental import pallas as pl
from jax.experimental.pallas import tpu as pltpu
from jax.sharding import PartitionSpec as P

distance_scale = 0.0625
margin = 1.0
pull_share = 0.5
BF = jnp.bfloat16
F32 = jnp.float32
BLOCK = 256
LANES = 128
NT = (((1,), (1,)), ((), ()))
NN = (((1,), (0,)), ((), ()))
PARAMS = pltpu.CompilerParams(vmem_limit_bytes=56 * 1024 * 1024)


def row_numbers():
    return lax.broadcasted_iota(jnp.int32, (BLOCK, LANES), 0).astype(F32).astype(BF)


def hits(index, base, numbers):
    place = (index - base).astype(F32).astype(BF)
    return [
        jnp.broadcast_to(place[:, c : c + LANES], (BLOCK, LANES)) == numbers
        for c in range(0, index.shape[1], LANES)
    ]


def select(mask, value):
    return jnp.where(mask, jnp.full((BLOCK, LANES), value, BF), jnp.zeros((BLOCK, LANES), BF))


def one_hot(index, base, rows, numbers, value=1.0):
    blocks = []
    for r in range(0, rows, BLOCK):
        blocks.append(
            jnp.concatenate([select(m, value) for m in hits(index, base + r, numbers)], axis=1)
        )
    return blocks[0] if len(blocks) == 1 else jnp.concatenate(blocks, axis=0)


def difference(anchor, other, rows, numbers):
    blocks = []
    for r in range(0, rows, BLOCK):
        pieces = [
            select(m, 1.0) - select(n, 1.0)
            for m, n in zip(hits(anchor, r, numbers), hits(other, r, numbers))
        ]
        blocks.append(jnp.concatenate(pieces, axis=1))
    return jnp.concatenate(blocks, axis=0)


def dot(a, b, contract=NN):
    return lax.dot_general(a, b, contract, preferred_element_type=F32)


def project_kernel(embeddings_ref, projection_ref, out_ref):
    out_ref[...] = dot(projection_ref[...], embeddings_ref[...], NT).astype(BF)


def serve_kernel(table_ref, wanted_ref, out_ref):
    numbers = row_numbers()
    groups, rank, slots = out_ref.shape
    step = 4

    def body(i, carry):
        first = i * step
        index = jnp.concatenate([wanted_ref[first + j] for j in range(step)], axis=1)
        served = dot(table_ref[...], one_hot(index, 0, table_ref.shape[1], numbers)).astype(BF)
        for j in range(step):
            out_ref[first + j] = served[:, j * slots : (j + 1) * slots]
        return carry

    lax.fori_loop(0, groups // step, body, 0)


def own_gather_kernel(table_ref, triplets_ref, positive_ref, negative_ref):
    numbers = row_numbers()
    rows = table_ref.shape[1]
    step = 512

    def body(i, carry):
        at = pl.ds(pl.multiple_of(i * step, step), step)
        anchor = triplets_ref[0:1, at]
        positive_ref[:, at] = dot(table_ref[...], difference(anchor, triplets_ref[1:2, at], rows, numbers))
        negative_ref[:, at] = dot(table_ref[...], difference(anchor, triplets_ref[2:3, at], rows, numbers))
        return carry

    lax.fori_loop(0, triplets_ref.shape[1] // step, body, 0)


def middle_kernel(fetched_ref, triplets_ref, cotangent_ref, positive_ref, negative_ref,
                  remote_ref, pull_ref, push_ref, table_ref, *, own):
    numbers = row_numbers()
    groups, rank, slots = fetched_ref.shape
    rows = groups * slots
    step = 512
    for g in range(groups):
        table_ref[:, g * slots : (g + 1) * slots] = fetched_ref[g]

    def gather(i, carry):
        at = pl.ds(pl.multiple_of(i * step, step), step)
        to_positive = positive_ref[:, at] - dot(
            table_ref[...], one_hot(triplets_ref[1:2, at], own, rows, numbers))
        to_negative = negative_ref[:, at] - dot(
            table_ref[...], one_hot(triplets_ref[2:3, at], own, rows, numbers))
        near = distance_scale * jnp.sum(to_positive * to_positive, axis=0, keepdims=True)
        far = distance_scale * jnp.sum(to_negative * to_negative, axis=0, keepdims=True)
        gate = jax.nn.sigmoid(margin + near - far)
        weight = cotangent_ref[:, at]
        pull = 2.0 * distance_scale * weight * (1.0 - pull_share + pull_share * gate)
        push = 2.0 * distance_scale * weight * pull_share * gate
        pull_ref[:, at] = (-pull * to_positive).astype(BF)
        push_ref[:, at] = (push * to_negative).astype(BF)
        return carry

    lax.fori_loop(0, triplets_ref.shape[1] // step, gather, 0)
    per = BLOCK // slots

    def scatter(i, carry):
        base = own + i * BLOCK
        total = dot(pull_ref[...], one_hot(triplets_ref[1:2, :], base, BLOCK, numbers), NT)
        total = total + dot(push_ref[...], one_hot(triplets_ref[2:3, :], base, BLOCK, numbers), NT)
        total = total.astype(BF)
        for j in range(per):
            remote_ref[i * per + j] = total[:, j * slots : (j + 1) * slots]
        return carry

    lax.fori_loop(0, rows // BLOCK, scatter, 0)


def own_scatter_kernel(pull_ref, push_ref, triplets_ref, out_ref):
    numbers = row_numbers()

    def body(i, carry):
        base = i * BLOCK
        anchor = hits(triplets_ref[0:1, :], base, numbers)
        parts = []
        for row in (1, 2):
            other = hits(triplets_ref[row : row + 1, :], base, numbers)
            parts.append(jnp.concatenate(
                [select(n, 1.0) - select(m, 1.0) for m, n in zip(anchor, other)], axis=1))
        total = dot(pull_ref[...], parts[0], NT) + dot(push_ref[...], parts[1], NT)
        out_ref[:, pl.ds(pl.multiple_of(base, BLOCK), BLOCK)] = total
        return carry

    lax.fori_loop(0, out_ref.shape[1] // BLOCK, body, 0)


def finish_kernel(own_ref, returned_ref, wanted_ref, embeddings_ref, rounded_ref, partial_ref, back_ref):
    numbers = row_numbers()
    groups, rank, slots = returned_ref.shape
    for g in range(groups):
        back_ref[:, g * slots : (g + 1) * slots] = returned_ref[g]
    index = jnp.concatenate([wanted_ref[g] for g in range(groups)], axis=1)

    def body(i, carry):
        at = pl.ds(pl.multiple_of(i * BLOCK, BLOCK), BLOCK)
        total = own_ref[:, at] + dot(back_ref[...], one_hot(index, i * BLOCK, BLOCK, numbers), NT)
        rounded_ref[:, at] = total.astype(BF)
        return carry

    lax.fori_loop(0, own_ref.shape[1] // BLOCK, body, 0)
    partial_ref[...] = dot(rounded_ref[...], embeddings_ref[...]).astype(partial_ref.dtype)


def shape(dims, kind):
    return jax.ShapeDtypeStruct(dims, kind)


def exchange(value, axis):
    return lax.all_to_all(value, axis, split_axis=0, concat_axis=0, tiled=True)


def reduce_all(partial, factor):
    groups, members = lax.axis_size("group"), lax.axis_size("dev")
    rank, width = partial.shape
    mine = exchange(partial.reshape(groups, rank // groups, width), "group")
    mine = jnp.sum(mine.astype(F32), axis=0)
    mine = mine.reshape(members, -1)
    mine = jnp.sum(exchange(mine, "dev"), axis=0) * factor
    mine = exchange(jnp.broadcast_to(mine[None], (members,) + mine.shape), "dev")
    mine = mine.reshape(rank // groups, width)
    whole = exchange(jnp.broadcast_to(mine[None], (groups,) + mine.shape), "group")
    return whole.reshape(rank, width)


def local(embeddings, projection, triplets, cotangent, wanted_rows):
    rows, width = embeddings.shape
    rank = projection.shape[0]
    count = triplets.shape[1]
    groups, slots = wanted_rows.shape
    wanted = exchange(wanted_rows.reshape(groups, 1, slots), "group")
    table = pl.pallas_call(project_kernel, out_shape=shape((rank, rows), BF),
                           compiler_params=PARAMS, name="project")(embeddings, projection)
    served = pl.pallas_call(serve_kernel, out_shape=shape((groups, rank, slots), BF),
                            compiler_params=PARAMS, name="serve")(table, wanted)
    fetched = exchange(served, "group")
    positive, negative = pl.pallas_call(
        own_gather_kernel, out_shape=[shape((rank, count), F32)] * 2,
        compiler_params=PARAMS, name="own_gather")(table, triplets)
    remote, pull, push = pl.pallas_call(
        functools.partial(middle_kernel, own=rows),
        out_shape=[shape((groups, rank, slots), BF), shape((rank, count), BF), shape((rank, count), BF)],
        scratch_shapes=[pltpu.VMEM((rank, groups * slots), BF)],
        compiler_params=PARAMS, name="middle",
    )(fetched, triplets, cotangent.reshape(1, count), positive, negative)
    returned = exchange(remote, "group")
    own = pl.pallas_call(own_scatter_kernel, out_shape=shape((rank, rows), F32),
                         compiler_params=PARAMS, name="own_scatter")(pull, push, triplets)
    rounded, partial = pl.pallas_call(
        finish_kernel,
        out_shape=[shape((rank, rows), BF), shape((rank, width), BF)],
        scratch_shapes=[pltpu.VMEM((rank, groups * slots), BF)],
        compiler_params=PARAMS, name="finish",
    )(own, returned, wanted, embeddings)
    factor = 1.0 / math.sqrt(cotangent.shape[0] * groups * lax.axis_size("dev"))
    weight_grad = reduce_all(partial, factor)
    row_grad = lax.dot_general(rounded, projection, (((0,), (0,)), ((), ())),
                               preferred_element_type=F32).astype(BF)
    return (row_grad, weight_grad)


def solution(mesh):
    return jax.shard_map(
        local,
        mesh=mesh,
        in_specs=(
            P(("group", "dev"), None),
            P(),
            P(None, ("group", "dev")),
            P(("group", "dev")),
            P(("group", "dev"), None),
        ),
        out_specs=(P(("group", "dev"), None), P()),
        check_vma=False,
    )
```

```python
import functools
import math

import jax
import jax.numpy as jnp
from jax import lax
from jax.experimental import pallas as pl
from jax.experimental.pallas import tpu as pltpu
from jax.sharding import PartitionSpec as P

distance_scale = 0.0625
margin = 1.0
pull_share = 0.5
BF = jnp.bfloat16
F32 = jnp.float32
BLOCK = 256
LANES = 128
NT = (((1,), (1,)), ((), ()))
NN = (((1,), (0,)), ((), ()))
PARAMS = pltpu.CompilerParams(vmem_limit_bytes=24 * 1024 * 1024)


def row_numbers():
    return lax.broadcasted_iota(jnp.int32, (BLOCK, LANES), 0).astype(F32).astype(BF)


def hits(index, base, numbers):
    place = (index - base).astype(F32).astype(BF)
    return [
        jnp.broadcast_to(place[:, c : c + LANES], (BLOCK, LANES)) == numbers
        for c in range(0, index.shape[1], LANES)
    ]


def select(mask, value):
    return jnp.where(mask, jnp.full((BLOCK, LANES), value, BF), jnp.zeros((BLOCK, LANES), BF))


def one_hot(index, base, rows, numbers, value=1.0):
    blocks = []
    for r in range(0, rows, BLOCK):
        blocks.append(
            jnp.concatenate([select(m, value) for m in hits(index, base + r, numbers)], axis=1)
        )
    return blocks[0] if len(blocks) == 1 else jnp.concatenate(blocks, axis=0)


def difference(anchor, other, rows, numbers):
    blocks = []
    for r in range(0, rows, BLOCK):
        pieces = [
            select(m, 1.0) - select(n, 1.0)
            for m, n in zip(hits(anchor, r, numbers), hits(other, r, numbers))
        ]
        blocks.append(jnp.concatenate(pieces, axis=1))
    return jnp.concatenate(blocks, axis=0)


def dot(a, b, contract=NN):
    return lax.dot_general(a, b, contract, preferred_element_type=F32)


def project_kernel(embeddings_ref, projection_ref, out_ref):
    out_ref[...] = dot(projection_ref[...], embeddings_ref[...], NT).astype(BF)


def serve_kernel(table_ref, wanted_ref, out_ref):
    numbers = row_numbers()
    groups, rank, slots = out_ref.shape
    step = 4
    for first in range(0, groups, step):
        index = jnp.concatenate([wanted_ref[first + j] for j in range(step)], axis=1)
        served = dot(table_ref[...], one_hot(index, 0, table_ref.shape[1], numbers)).astype(BF)
        for j in range(step):
            out_ref[first + j] = served[:, j * slots : (j + 1) * slots]


def own_gather_kernel(table_ref, triplets_ref, positive_ref, negative_ref):
    numbers = row_numbers()
    rows = table_ref.shape[1]
    step = 512
    for i in range(0, triplets_ref.shape[1], step):
        at = pl.ds(i, step)
        anchor = triplets_ref[0:1, at]
        positive_ref[:, at] = dot(table_ref[...], difference(anchor, triplets_ref[1:2, at], rows, numbers))
        negative_ref[:, at] = dot(table_ref[...], difference(anchor, triplets_ref[2:3, at], rows, numbers))


def middle_kernel(fetched_ref, triplets_ref, cotangent_ref, positive_hbm, negative_hbm,
                  remote_ref, pull_hbm, push_hbm,
                  table_ref, positive_ref, negative_ref, pull_ref, push_ref, arrived, left, *, own):
    incoming = [pltpu.make_async_copy(positive_hbm, positive_ref, arrived.at[0]),
                pltpu.make_async_copy(negative_hbm, negative_ref, arrived.at[1])]
    outgoing = [pltpu.make_async_copy(pull_ref, pull_hbm, left.at[0]),
                pltpu.make_async_copy(push_ref, push_hbm, left.at[1])]
    for copy in incoming:
        copy.start()
    numbers = row_numbers()
    groups, rank, slots = fetched_ref.shape
    rows = groups * slots
    step = 512
    for g in range(groups):
        table_ref[:, g * slots : (g + 1) * slots] = fetched_ref[g]
    for i in range(0, triplets_ref.shape[1], step):
        at = pl.ds(i, step)
        positive = dot(table_ref[...], one_hot(triplets_ref[1:2, at], own, rows, numbers))
        negative = dot(table_ref[...], one_hot(triplets_ref[2:3, at], own, rows, numbers))
        if i == 0:
            for copy in incoming:
                copy.wait()
        to_positive = positive_ref[:, at] - positive
        to_negative = negative_ref[:, at] - negative
        near = distance_scale * jnp.sum(to_positive * to_positive, axis=0, keepdims=True)
        far = distance_scale * jnp.sum(to_negative * to_negative, axis=0, keepdims=True)
        gate = jax.nn.sigmoid(margin + near - far)
        weight = cotangent_ref[:, at]
        pull = 2.0 * distance_scale * weight * (1.0 - pull_share + pull_share * gate)
        push = 2.0 * distance_scale * weight * pull_share * gate
        pull_ref[:, at] = (-pull * to_positive).astype(BF)
        push_ref[:, at] = (push * to_negative).astype(BF)
    for copy in outgoing:
        copy.start()
    per = step // slots
    for i in range(rows // step):
        base = own + i * step
        total = dot(pull_ref[...], one_hot(triplets_ref[1:2, :], base, step, numbers), NT)
        total = total + dot(push_ref[...], one_hot(triplets_ref[2:3, :], base, step, numbers), NT)
        total = total.astype(BF)
        for j in range(per):
            remote_ref[i * per + j] = total[:, j * slots : (j + 1) * slots]
    for copy in outgoing:
        copy.wait()


def own_scatter_kernel(pull_ref, push_ref, triplets_ref, out_ref):
    numbers = row_numbers()
    for base in range(0, out_ref.shape[1], BLOCK):
        anchor = hits(triplets_ref[0:1, :], base, numbers)
        parts = []
        for row in (1, 2):
            other = hits(triplets_ref[row : row + 1, :], base, numbers)
            parts.append(jnp.concatenate(
                [select(n, 1.0) - select(m, 1.0) for m, n in zip(anchor, other)], axis=1))
        out_ref[:, pl.ds(base, BLOCK)] = dot(pull_ref[...], parts[0], NT) + dot(push_ref[...], parts[1], NT)


def finish_kernel(side_ref, own_hbm, returned_ref, wanted_ref, embeddings_hbm,
                  rounded_ref, kept_ref, sent_ref, back_ref, own_ref, embeddings_ref, arrived):
    own_copy = pltpu.make_async_copy(own_hbm, own_ref, arrived.at[0])
    embeddings_copy = pltpu.make_async_copy(embeddings_hbm, embeddings_ref, arrived.at[1])
    own_copy.start()
    embeddings_copy.start()
    numbers = row_numbers()
    groups, rank, slots = returned_ref.shape
    for g in range(groups):
        back_ref[:, g * slots : (g + 1) * slots] = returned_ref[g]
    index = jnp.concatenate([wanted_ref[g] for g in range(groups)], axis=1)
    for base in range(0, own_ref.shape[1], BLOCK):
        at = pl.ds(base, BLOCK)
        total = dot(back_ref[...], one_hot(index, base, BLOCK, numbers), NT)
        if base == 0:
            own_copy.wait()
        rounded_ref[:, at] = (own_ref[:, at] + total).astype(BF)
    embeddings_copy.wait()
    half = rank // 2
    side = side_ref[0]
    mine = pl.multiple_of(side * half, half)
    theirs = pl.multiple_of((1 - side) * half, half)
    sent_ref[...] = dot(rounded_ref[pl.ds(theirs, half), :], embeddings_ref[...])
    kept_ref[...] = dot(rounded_ref[pl.ds(mine, half), :], embeddings_ref[...])


def pair_kernel(kept_ref, received_ref, out_ref):
    groups, part, width = out_ref.shape
    total = kept_ref[...] + received_ref[...]
    out_ref[...] = total.reshape(groups, part, width).astype(BF)


def spread_kernel(parts_ref, out_ref, *, factor):
    total = parts_ref[0].astype(F32)
    for g in range(1, parts_ref.shape[0]):
        total = total + parts_ref[g].astype(F32)
    total = (total * factor).astype(out_ref.dtype)
    for g in range(out_ref.shape[0]):
        out_ref[g] = total


def join_kernel(side_ref, mine_ref, theirs_ref, out_hbm, left):
    half = mine_ref.shape[0]
    side = side_ref[0]
    copies = []
    for i, (source, start) in enumerate([(mine_ref, side * half), (theirs_ref, (1 - side) * half)]):
        target = out_hbm.at[pl.ds(pl.multiple_of(start, half), half), :]
        copies.append(pltpu.make_async_copy(source, target, left.at[i]))
    for copy in copies:
        copy.start()
    for copy in copies:
        copy.wait()


NEAR, FAR, PLAIN, SCALAR = "near", "far", "plain", "scalar"
SPACES = {NEAR: pltpu.VMEM, FAR: pltpu.HBM, PLAIN: pltpu.HBM}
SPECS = {
    NEAR: pl.BlockSpec(memory_space=pltpu.VMEM),
    FAR: pl.BlockSpec(memory_space=pltpu.HBM),
    PLAIN: pl.BlockSpec(memory_space=pltpu.VMEM),
    SCALAR: pl.BlockSpec(memory_space=pltpu.SMEM),
}


def call(kernel, name, outs, ins, scratch=()):
    args = [a if place == SCALAR else pltpu.with_memory_space_constraint(a, SPACES[place]) for place, a in ins]
    shapes = [SPACES[place](dims, kind) for place, dims, kind in outs]
    result = pl.pallas_call(
        kernel, out_shape=shapes, in_specs=[SPECS[place] for place, _ in ins],
        out_specs=[SPECS[out[0]] for out in outs], scratch_shapes=scratch,
        compiler_params=PARAMS, name=name)(*args)
    return result if len(outs) > 1 else result[0]


def exchange(value, axis, groups=None):
    return lax.all_to_all(value, axis, split_axis=0, concat_axis=0, tiled=True, axis_index_groups=groups)


def local(embeddings, projection, triplets, cotangent, wanted_rows):
    rows, width = embeddings.shape
    rank = projection.shape[0]
    count = triplets.shape[1]
    groups, slots = wanted_rows.shape
    members = lax.axis_size("dev")
    cores = 2
    levels = members // cores
    half = rank // cores
    part = half // groups
    side = (lax.axis_index("dev") & 1).astype(jnp.int32).reshape(1)
    swap = [(i, i ^ 1) for i in range(members)]
    column = [[cores * z + c for z in range(levels)] for c in range(cores)]
    factor = 1.0 / math.sqrt(cotangent.shape[0] * groups * members)
    requests = groups * slots
    two = pltpu.SemaphoreType.DMA((2,))

    wanted = exchange(wanted_rows.reshape(groups, 1, slots), "group")
    table = call(project_kernel, "project", [(NEAR, (rank, rows), BF)],
                 [(NEAR, embeddings), (NEAR, projection)])
    served = call(serve_kernel, "serve", [(NEAR, (groups, rank, slots), BF)], [(NEAR, table), (NEAR, wanted)])
    fetched = exchange(served, "group")
    positive, negative = call(own_gather_kernel, "own_gather", [(PLAIN, (rank, count), F32)] * 2,
                              [(NEAR, table), (NEAR, triplets)])
    remote, pull, push = call(
        functools.partial(middle_kernel, own=rows), "middle",
        [(NEAR, (groups, rank, slots), BF), (FAR, (rank, count), BF), (FAR, (rank, count), BF)],
        [(NEAR, fetched), (NEAR, triplets), (NEAR, cotangent.reshape(1, count)), (FAR, positive), (FAR, negative)],
        [pltpu.VMEM((rank, requests), BF)] + [pltpu.VMEM((rank, count), F32)] * 2
        + [pltpu.VMEM((rank, count), BF)] * 2 + [two, two])
    returned = exchange(remote, "group")
    own = call(own_scatter_kernel, "own_scatter", [(PLAIN, (rank, rows), F32)],
               [(PLAIN, pull), (PLAIN, push), (NEAR, triplets)])
    rounded, kept, sent = call(
        finish_kernel, "finish",
        [(NEAR, (rank, rows), BF), (NEAR, (half, width), F32), (NEAR, (half, width), F32)],
        [(SCALAR, side), (FAR, own), (NEAR, returned), (NEAR, wanted), (FAR, embeddings)],
        [pltpu.VMEM((rank, requests), BF), pltpu.VMEM((rank, rows), F32), pltpu.VMEM((rows, width), BF), two])
    received = lax.ppermute(sent, "dev", swap)
    chip = call(pair_kernel, "pair", [(NEAR, (groups, part, width), BF)], [(NEAR, kept), (NEAR, received)])
    chip = exchange(chip, "group")
    plane = call(functools.partial(spread_kernel, factor=1.0), "plane",
                 [(NEAR, (levels, part, width), BF)], [(NEAR, chip)])
    plane = exchange(plane, "dev", column)
    whole = call(functools.partial(spread_kernel, factor=factor), "whole",
                 [(NEAR, (groups, part, width), F32)], [(NEAR, plane)])
    mine = exchange(whole, "group").reshape(half, width)
    theirs = lax.ppermute(mine, "dev", swap)
    weight_grad = call(join_kernel, "join", [(FAR, (rank, width), F32)],
                       [(SCALAR, side), (NEAR, mine), (NEAR, theirs)], [two])
    row_grad = lax.dot_general(rounded, projection, (((0,), (0,)), ((), ())),
                               preferred_element_type=F32).astype(BF)
    return (row_grad, weight_grad)


def solution(mesh):
    return jax.shard_map(
        local,
        mesh=mesh,
        in_specs=(
            P(("group", "dev"), None),
            P(),
            P(None, ("group", "dev")),
            P(("group", "dev")),
            P(("group", "dev"), None),
        ),
        out_specs=(P(("group", "dev"), None), P()),
        check_vma=False,
    )
```

```python
import functools
import math

import jax
import jax.numpy as jnp
from jax import lax
from jax.experimental import pallas as pl
from jax.experimental.pallas import tpu as pltpu
from jax.sharding import PartitionSpec as P

distance_scale = 0.0625
margin = 1.0
pull_share = 0.5
BF = jnp.bfloat16
F32 = jnp.float32
BLOCK = 256
LANES = 128
NT = (((1,), (1,)), ((), ()))
NN = (((1,), (0,)), ((), ()))
PARAMS = pltpu.CompilerParams(vmem_limit_bytes=24 * 1024 * 1024)


def row_numbers():
    return lax.broadcasted_iota(jnp.int32, (BLOCK, LANES), 0).astype(F32).astype(BF)


def hits(index, base, numbers):
    place = (index - base).astype(F32).astype(BF)
    return [
        jnp.broadcast_to(place[:, c : c + LANES], (BLOCK, LANES)) == numbers
        for c in range(0, index.shape[1], LANES)
    ]


def select(mask, value):
    return jnp.where(mask, jnp.full((BLOCK, LANES), value, BF), jnp.zeros((BLOCK, LANES), BF))


def one_hot(index, base, rows, numbers, value=1.0):
    blocks = []
    for r in range(0, rows, BLOCK):
        blocks.append(
            jnp.concatenate([select(m, value) for m in hits(index, base + r, numbers)], axis=1)
        )
    return blocks[0] if len(blocks) == 1 else jnp.concatenate(blocks, axis=0)


def difference(anchor, other, rows, numbers):
    blocks = []
    for r in range(0, rows, BLOCK):
        pieces = [
            select(m, 1.0) - select(n, 1.0)
            for m, n in zip(hits(anchor, r, numbers), hits(other, r, numbers))
        ]
        blocks.append(jnp.concatenate(pieces, axis=1))
    return jnp.concatenate(blocks, axis=0)


def dot(a, b, contract=NN):
    return lax.dot_general(a, b, contract, preferred_element_type=F32)


def project_kernel(embeddings_ref, projection_ref, out_ref):
    out_ref[...] = dot(projection_ref[...], embeddings_ref[...], NT).astype(BF)


def serve_kernel(table_ref, wanted_ref, out_hbm, out_ref, left):
    numbers = row_numbers()
    groups, rank, slots = out_ref.shape
    step = groups // 4
    copies = []
    for i in range(4):
        first = i * step
        index = jnp.concatenate([wanted_ref[first + j] for j in range(step)], axis=1)
        served = dot(table_ref[...], one_hot(index, 0, table_ref.shape[1], numbers)).astype(BF)
        for j in range(step):
            out_ref[first + j] = served[:, j * slots : (j + 1) * slots]
        some = pl.ds(first, step)
        copies.append(pltpu.make_async_copy(out_ref.at[some], out_hbm.at[some], left.at[i]))
        copies[-1].start()
    for copy in copies:
        copy.wait()


def own_gather_kernel(table_ref, triplets_ref, positive_ref, negative_ref):
    numbers = row_numbers()
    rows = table_ref.shape[1]
    step = 512
    for i in range(0, triplets_ref.shape[1], step):
        at = pl.ds(i, step)
        anchor = triplets_ref[0:1, at]
        positive_ref[:, at] = dot(table_ref[...], difference(anchor, triplets_ref[1:2, at], rows, numbers))
        negative_ref[:, at] = dot(table_ref[...], difference(anchor, triplets_ref[2:3, at], rows, numbers))


def middle_kernel(fetched_ref, triplets_ref, cotangent_ref, positive_hbm, negative_hbm,
                  remote_hbm, pull_hbm, push_hbm,
                  table_ref, positive_ref, negative_ref, remote_ref, pull_ref, push_ref,
                  arrived, left, sent, *, own):
    numbers = row_numbers()
    groups, rank, slots = fetched_ref.shape
    rows = groups * slots
    count = triplets_ref.shape[1]
    parts = 4
    step = count // parts
    incoming = []
    for i in range(parts):
        at = pl.ds(i * step, step)
        incoming.append([
            pltpu.make_async_copy(positive_hbm.at[:, at], positive_ref.at[:, at], arrived.at[2 * i]),
            pltpu.make_async_copy(negative_hbm.at[:, at], negative_ref.at[:, at], arrived.at[2 * i + 1])])
        for copy in incoming[-1]:
            copy.start()
    outgoing = [pltpu.make_async_copy(pull_ref, pull_hbm, left.at[0]),
                pltpu.make_async_copy(push_ref, push_hbm, left.at[1])]
    for g in range(groups):
        table_ref[:, g * slots : (g + 1) * slots] = fetched_ref[g]
    for i in range(parts):
        at = pl.ds(i * step, step)
        positive = dot(table_ref[...], one_hot(triplets_ref[1:2, at], own, rows, numbers))
        negative = dot(table_ref[...], one_hot(triplets_ref[2:3, at], own, rows, numbers))
        for copy in incoming[i]:
            copy.wait()
        to_positive = positive_ref[:, at] - positive
        to_negative = negative_ref[:, at] - negative
        near = distance_scale * jnp.sum(to_positive * to_positive, axis=0, keepdims=True)
        far = distance_scale * jnp.sum(to_negative * to_negative, axis=0, keepdims=True)
        gate = jax.nn.sigmoid(margin + near - far)
        weight = cotangent_ref[:, at]
        pull = 2.0 * distance_scale * weight * (1.0 - pull_share + pull_share * gate)
        push = 2.0 * distance_scale * weight * pull_share * gate
        pull_ref[:, at] = (-pull * to_positive).astype(BF)
        push_ref[:, at] = (push * to_negative).astype(BF)
    for copy in outgoing:
        copy.start()
    step = rows // parts
    per = step // slots
    for i in range(parts):
        base = own + i * step
        total = dot(pull_ref[...], one_hot(triplets_ref[1:2, :], base, step, numbers), NT)
        total = total + dot(push_ref[...], one_hot(triplets_ref[2:3, :], base, step, numbers), NT)
        total = total.astype(BF)
        for j in range(per):
            remote_ref[i * per + j] = total[:, j * slots : (j + 1) * slots]
        some = pl.ds(i * per, per)
        outgoing.append(pltpu.make_async_copy(remote_ref.at[some], remote_hbm.at[some], sent.at[i]))
        outgoing[-1].start()
    for copy in outgoing:
        copy.wait()


def own_scatter_kernel(pull_ref, push_ref, triplets_ref, out_ref):
    numbers = row_numbers()
    for base in range(0, out_ref.shape[1], BLOCK):
        anchor = hits(triplets_ref[0:1, :], base, numbers)
        parts = []
        for row in (1, 2):
            other = hits(triplets_ref[row : row + 1, :], base, numbers)
            parts.append(jnp.concatenate(
                [select(n, 1.0) - select(m, 1.0) for m, n in zip(anchor, other)], axis=1))
        out_ref[:, pl.ds(base, BLOCK)] = dot(pull_ref[...], parts[0], NT) + dot(push_ref[...], parts[1], NT)


def finish_kernel(own_hbm, returned_ref, wanted_ref, embeddings_hbm,
                  rounded_ref, partial_ref, back_ref, own_ref, embeddings_ref, arrived):
    numbers = row_numbers()
    groups, rank, slots = returned_ref.shape
    rows = own_ref.shape[1]
    owns = []
    for i, base in enumerate(range(0, rows, BLOCK)):
        at = pl.ds(base, BLOCK)
        owns.append(pltpu.make_async_copy(own_hbm.at[:, at], own_ref.at[:, at], arrived.at[i + 1]))
        owns[-1].start()
    embeddings_copy = pltpu.make_async_copy(embeddings_hbm, embeddings_ref, arrived.at[0])
    embeddings_copy.start()
    for g in range(groups):
        back_ref[:, g * slots : (g + 1) * slots] = returned_ref[g]
    index = jnp.concatenate([wanted_ref[g] for g in range(groups)], axis=1)
    for i, base in enumerate(range(0, rows, BLOCK)):
        at = pl.ds(base, BLOCK)
        total = dot(back_ref[...], one_hot(index, base, BLOCK, numbers), NT)
        owns[i].wait()
        rounded_ref[:, at] = (own_ref[:, at] + total).astype(BF)
    embeddings_copy.wait()
    partial = dot(rounded_ref[...], embeddings_ref[...])
    partial_ref[...] = partial.reshape(partial_ref.shape).astype(BF)


def spread_kernel(parts_ref, out_ref, *, factor):
    total = parts_ref[0].astype(F32)
    for g in range(1, parts_ref.shape[0]):
        total = total + parts_ref[g].astype(F32)
    total = (total * factor).astype(out_ref.dtype)
    for g in range(out_ref.shape[0]):
        out_ref[g] = total


def widen_kernel(parts_ref, out_ref):
    out_ref[...] = parts_ref[...].astype(F32).reshape(out_ref.shape)


NEAR, FAR, PLAIN, SCALAR = "near", "far", "plain", "scalar"
SPACES = {NEAR: pltpu.VMEM, FAR: pltpu.HBM, PLAIN: pltpu.HBM}
SPECS = {
    NEAR: pl.BlockSpec(memory_space=pltpu.VMEM),
    FAR: pl.BlockSpec(memory_space=pltpu.HBM),
    PLAIN: pl.BlockSpec(memory_space=pltpu.VMEM),
    SCALAR: pl.BlockSpec(memory_space=pltpu.SMEM),
}


def call(kernel, name, outs, ins, scratch=()):
    args = [a if place == SCALAR else pltpu.with_memory_space_constraint(a, SPACES[place]) for place, a in ins]
    shapes = [SPACES[place](dims, kind) for place, dims, kind in outs]
    result = pl.pallas_call(
        kernel, out_shape=shapes, in_specs=[SPECS[place] for place, _ in ins],
        out_specs=[SPECS[out[0]] for out in outs], scratch_shapes=scratch,
        compiler_params=PARAMS, name=name)(*args)
    return result if len(outs) > 1 else result[0]


def exchange(value, axis, groups=None):
    return lax.all_to_all(value, axis, split_axis=0, concat_axis=0, tiled=True, axis_index_groups=groups)


def local(embeddings, projection, triplets, cotangent, wanted_rows):
    rows, width = embeddings.shape
    rank = projection.shape[0]
    count = triplets.shape[1]
    groups, slots = wanted_rows.shape
    members = lax.axis_size("dev")
    cores = 2
    levels = members // cores
    near = groups * cores
    part = rank // near
    level = [[g * members + cores * z + c for g in range(groups) for c in range(cores)] for z in range(levels)]
    column = [[cores * z + c for z in range(levels)] for c in range(cores)]
    factor = 1.0 / math.sqrt(cotangent.shape[0] * groups * members)
    requests = groups * slots
    blocks = rows // BLOCK

    def arrivals(n):
        return pltpu.SemaphoreType.DMA((n,))

    wanted = exchange(wanted_rows.reshape(groups, 1, slots), "group")
    table = call(project_kernel, "project", [(NEAR, (rank, rows), BF)],
                 [(NEAR, embeddings), (NEAR, projection)])
    served = call(serve_kernel, "serve", [(FAR, (groups, rank, slots), BF)], [(NEAR, table), (NEAR, wanted)],
                  [pltpu.VMEM((groups, rank, slots), BF), arrivals(4)])
    fetched = exchange(served, "group")
    positive, negative = call(own_gather_kernel, "own_gather", [(PLAIN, (rank, count), F32)] * 2,
                              [(NEAR, table), (NEAR, triplets)])
    remote, pull, push = call(
        functools.partial(middle_kernel, own=rows), "middle",
        [(FAR, (groups, rank, slots), BF), (FAR, (rank, count), BF), (FAR, (rank, count), BF)],
        [(NEAR, fetched), (NEAR, triplets), (NEAR, cotangent.reshape(1, count)), (FAR, positive), (FAR, negative)],
        [pltpu.VMEM((rank, requests), BF)] + [pltpu.VMEM((rank, count), F32)] * 2
        + [pltpu.VMEM((groups, rank, slots), BF)] + [pltpu.VMEM((rank, count), BF)] * 2
        + [arrivals(8), arrivals(2), arrivals(4)])
    returned = exchange(remote, "group")
    own = call(own_scatter_kernel, "own_scatter", [(PLAIN, (rank, rows), F32)],
               [(PLAIN, pull), (PLAIN, push), (NEAR, triplets)])
    rounded, partial = call(
        finish_kernel, "finish",
        [(NEAR, (rank, rows), BF), (NEAR, (near, part, width), BF)],
        [(FAR, own), (NEAR, returned), (NEAR, wanted), (FAR, embeddings)],
        [pltpu.VMEM((rank, requests), BF), pltpu.VMEM((rank, rows), F32), pltpu.VMEM((rows, width), BF),
         arrivals(blocks + 1)])
    plane = exchange(partial, ("group", "dev"), level)
    plane = call(functools.partial(spread_kernel, factor=1.0), "plane",
                 [(NEAR, (levels, part, width), BF)], [(NEAR, plane)])
    whole = exchange(plane, "dev", column)
    whole = call(functools.partial(spread_kernel, factor=factor), "whole",
                 [(NEAR, (near, part, width), BF)], [(NEAR, whole)])
    whole = exchange(whole, ("group", "dev"), level)
    weight_grad = call(widen_kernel, "widen", [(PLAIN, (rank, width), F32)], [(NEAR, whole)])
    row_grad = lax.dot_general(rounded, projection, (((0,), (0,)), ((), ())),
                               preferred_element_type=F32).astype(BF)
    return (row_grad, weight_grad)


def solution(mesh):
    return jax.shard_map(
        local,
        mesh=mesh,
        in_specs=(
            P(("group", "dev"), None),
            P(),
            P(None, ("group", "dev")),
            P(("group", "dev")),
            P(("group", "dev"), None),
        ),
        out_specs=(P(("group", "dev"), None), P()),
        check_vma=False,
    )
```

```python
import functools
import math

import jax
import jax.numpy as jnp
from jax import lax
from jax.experimental import pallas as pl
from jax.experimental.pallas import tpu as pltpu
from jax.sharding import PartitionSpec as P

distance_scale = 0.0625
margin = 1.0
pull_share = 0.5
BF = jnp.bfloat16
F32 = jnp.float32
BLOCK = 256
LANES = 128
NT = (((1,), (1,)), ((), ()))
NN = (((1,), (0,)), ((), ()))
PARAMS = pltpu.CompilerParams(vmem_limit_bytes=24 * 1024 * 1024)


def row_numbers():
    return lax.broadcasted_iota(jnp.int32, (BLOCK, LANES), 0).astype(F32).astype(BF)


def hits(index, base, numbers):
    place = (index - base).astype(F32).astype(BF)
    return [
        jnp.broadcast_to(place[:, c : c + LANES], (BLOCK, LANES)) == numbers
        for c in range(0, index.shape[1], LANES)
    ]


def select(mask, value):
    return jnp.where(mask, jnp.full((BLOCK, LANES), value, BF), jnp.zeros((BLOCK, LANES), BF))


def one_hot(index, base, rows, numbers, value=1.0):
    blocks = []
    for r in range(0, rows, BLOCK):
        blocks.append(
            jnp.concatenate([select(m, value) for m in hits(index, base + r, numbers)], axis=1)
        )
    return blocks[0] if len(blocks) == 1 else jnp.concatenate(blocks, axis=0)


def dot(a, b, contract=NN):
    return lax.dot_general(a, b, contract, preferred_element_type=F32)


def project_kernel(embeddings_ref, projection_ref, out_ref, out_hbm, left):
    out_ref[...] = dot(projection_ref[...], embeddings_ref[...], NT).astype(BF)
    copy = pltpu.make_async_copy(out_ref, out_hbm, left.at[0])
    copy.start()
    copy.wait()


def serve_kernel(table_ref, wanted_ref, out_hbm, out_ref, left):
    numbers = row_numbers()
    groups, rank, slots = out_ref.shape
    step = groups // 4
    copies = []
    for i in range(4):
        first = i * step
        index = jnp.concatenate([wanted_ref[first + j] for j in range(step)], axis=1)
        served = dot(table_ref[...], one_hot(index, 0, table_ref.shape[1], numbers)).astype(BF)
        for j in range(step):
            out_ref[first + j] = served[:, j * slots : (j + 1) * slots]
        some = pl.ds(first, step)
        copies.append(pltpu.make_async_copy(out_ref.at[some], out_hbm.at[some], left.at[i]))
        copies[-1].start()
    for copy in copies:
        copy.wait()


def own_gather_kernel(table_ref, triplets_ref, anchor_ref, positive_ref, negative_hbm, negative_ref, left):
    numbers = row_numbers()
    rows = table_ref.shape[1]
    step = 512
    copy = pltpu.make_async_copy(negative_ref, negative_hbm, left.at[0])
    for row, out_ref in ((2, negative_ref), (0, anchor_ref), (1, positive_ref)):
        for i in range(0, triplets_ref.shape[1], step):
            at = pl.ds(i, step)
            out_ref[:, at] = dot(table_ref[...], one_hot(triplets_ref[row : row + 1, at], 0, rows, numbers)).astype(BF)
        if row == 2:
            copy.start()
    copy.wait()


def middle_kernel(fetched_ref, triplets_ref, cotangent_ref, anchor_ref, positive_ref, negative_hbm,
                  remote_hbm, pull_hbm, push_hbm,
                  table_ref, negative_ref, remote_ref, pull_ref, push_ref,
                  arrived, left, sent, *, own):
    numbers = row_numbers()
    groups, rank, slots = fetched_ref.shape
    rows = groups * slots
    count = triplets_ref.shape[1]
    parts = 4
    step = count // parts
    incoming = pltpu.make_async_copy(negative_hbm, negative_ref, arrived.at[0])
    incoming.start()
    outgoing = [pltpu.make_async_copy(pull_ref, pull_hbm, left.at[0]),
                pltpu.make_async_copy(push_ref, push_hbm, left.at[1])]
    for g in range(groups):
        table_ref[:, g * slots : (g + 1) * slots] = fetched_ref[g]
    for i in range(parts):
        at = pl.ds(i * step, step)
        positive = dot(table_ref[...], one_hot(triplets_ref[1:2, at], own, rows, numbers))
        negative = dot(table_ref[...], one_hot(triplets_ref[2:3, at], own, rows, numbers))
        if i == 0:
            incoming.wait()
        anchor = anchor_ref[:, at].astype(F32)
        to_positive = anchor - (positive_ref[:, at].astype(F32) + positive)
        to_negative = anchor - (negative_ref[:, at].astype(F32) + negative)
        near = distance_scale * jnp.sum(to_positive * to_positive, axis=0, keepdims=True)
        far = distance_scale * jnp.sum(to_negative * to_negative, axis=0, keepdims=True)
        gate = jax.nn.sigmoid(margin + near - far)
        weight = cotangent_ref[:, at]
        pull = 2.0 * distance_scale * weight * (1.0 - pull_share + pull_share * gate)
        push = 2.0 * distance_scale * weight * pull_share * gate
        pull_ref[:, at] = (-pull * to_positive).astype(BF)
        push_ref[:, at] = (push * to_negative).astype(BF)
    for copy in outgoing:
        copy.start()
    step = rows // parts
    per = step // slots
    for i in range(parts):
        base = own + i * step
        total = dot(pull_ref[...], one_hot(triplets_ref[1:2, :], base, step, numbers), NT)
        total = total + dot(push_ref[...], one_hot(triplets_ref[2:3, :], base, step, numbers), NT)
        total = total.astype(BF)
        for j in range(per):
            remote_ref[i * per + j] = total[:, j * slots : (j + 1) * slots]
        some = pl.ds(i * per, per)
        outgoing.append(pltpu.make_async_copy(remote_ref.at[some], remote_hbm.at[some], sent.at[i]))
        outgoing[-1].start()
    for copy in outgoing:
        copy.wait()


def own_scatter_kernel(pull_ref, push_ref, triplets_ref, out_ref):
    numbers = row_numbers()
    for base in range(0, out_ref.shape[1], BLOCK):
        anchor = hits(triplets_ref[0:1, :], base, numbers)
        parts = []
        for row in (1, 2):
            other = hits(triplets_ref[row : row + 1, :], base, numbers)
            parts.append(jnp.concatenate(
                [select(n, 1.0) - select(m, 1.0) for m, n in zip(anchor, other)], axis=1))
        out_ref[:, pl.ds(base, BLOCK)] = dot(pull_ref[...], parts[0], NT) + dot(push_ref[...], parts[1], NT)


def finish_kernel(on_ref, own_ref, returned_ref, wanted_ref, embeddings_hbm,
                  rounded_ref, partial_ref, back_ref, embeddings_ref, arrived):
    numbers = row_numbers()
    groups, rank, slots = returned_ref.shape
    copy = pltpu.make_async_copy(embeddings_hbm, embeddings_ref, arrived.at[0])
    copy.start()

    @pl.when(on_ref[0] >= 0)
    def _():
        for g in range(groups):
            back_ref[:, g * slots : (g + 1) * slots] = returned_ref[g]
        index = jnp.concatenate([wanted_ref[g] for g in range(groups)], axis=1)
        for base in range(0, own_ref.shape[1], BLOCK):
            at = pl.ds(base, BLOCK)
            total = dot(back_ref[...], one_hot(index, base, BLOCK, numbers), NT)
            rounded_ref[:, at] = (own_ref[:, at] + total).astype(BF)

    copy.wait()
    partial_ref[...] = dot(rounded_ref[...], embeddings_ref[...]).astype(BF)


def spread_kernel(parts_ref, out_ref, *, factor):
    total = parts_ref[0].astype(F32)
    for g in range(1, parts_ref.shape[0]):
        total = total + parts_ref[g].astype(F32)
    total = (total * factor).astype(out_ref.dtype)
    for g in range(out_ref.shape[0]):
        out_ref[g] = total


def widen_kernel(parts_ref, out_ref):
    out_ref[...] = parts_ref[...].astype(F32)


NEAR, FAR, PLAIN, SCALAR = "near", "far", "plain", "scalar"
SPACES = {NEAR: pltpu.VMEM, FAR: pltpu.HBM, PLAIN: pltpu.HBM}
SPECS = {
    NEAR: pl.BlockSpec(memory_space=pltpu.VMEM),
    FAR: pl.BlockSpec(memory_space=pltpu.HBM),
    PLAIN: pl.BlockSpec(memory_space=pltpu.VMEM),
    SCALAR: pl.BlockSpec(memory_space=pltpu.SMEM),
}


def call(kernel, name, outs, ins, scratch=()):
    args = [a if place == SCALAR else pltpu.with_memory_space_constraint(a, SPACES[place]) for place, a in ins]
    shapes = [SPACES[place](dims, kind) for place, dims, kind in outs]
    result = pl.pallas_call(
        kernel, out_shape=shapes, in_specs=[SPECS[place] for place, _ in ins],
        out_specs=[SPECS[out[0]] for out in outs], scratch_shapes=scratch,
        compiler_params=PARAMS, name=name)(*args)
    return result if len(outs) > 1 else result[0]


def exchange(value, axis, groups=None):
    return lax.all_to_all(value, axis, split_axis=0, concat_axis=0, tiled=True, axis_index_groups=groups)


def local(embeddings, projection, triplets, cotangent, wanted_rows):
    rows, width = embeddings.shape
    rank = projection.shape[0]
    count = triplets.shape[1]
    groups, slots = wanted_rows.shape
    members = lax.axis_size("dev")
    cores = 2
    levels = members // cores
    near = groups * cores
    part = rank // near
    level = [[g * members + cores * z + c for g in range(groups) for c in range(cores)] for z in range(levels)]
    column = [[cores * z + c for z in range(levels)] for c in range(cores)]
    factor = 1.0 / math.sqrt(cotangent.shape[0] * groups * members)
    requests = groups * slots
    on = lax.axis_index("dev").astype(jnp.int32).reshape(1)

    def arrivals(n):
        return pltpu.SemaphoreType.DMA((n,))

    wanted = exchange(wanted_rows.reshape(groups, 1, slots), "group")
    table, table_hbm = call(project_kernel, "project", [(NEAR, (rank, rows), BF), (FAR, (rank, rows), BF)],
                            [(NEAR, embeddings), (NEAR, projection)], [arrivals(1)])
    served = call(serve_kernel, "serve", [(FAR, (groups, rank, slots), BF)], [(NEAR, table), (NEAR, wanted)],
                  [pltpu.VMEM((groups, rank, slots), BF), arrivals(4)])
    fetched = exchange(served, "group")
    anchor, positive, negative = call(
        own_gather_kernel, "own_gather",
        [(NEAR, (rank, count), BF), (NEAR, (rank, count), BF), (FAR, (rank, count), BF)],
        [(PLAIN, table_hbm), (NEAR, triplets)], [pltpu.VMEM((rank, count), BF), arrivals(1)])
    remote, pull, push = call(
        functools.partial(middle_kernel, own=rows), "middle",
        [(FAR, (groups, rank, slots), BF), (FAR, (rank, count), BF), (FAR, (rank, count), BF)],
        [(NEAR, fetched), (NEAR, triplets), (NEAR, cotangent.reshape(1, count)),
         (NEAR, anchor), (NEAR, positive), (FAR, negative)],
        [pltpu.VMEM((rank, requests), BF), pltpu.VMEM((rank, count), BF), pltpu.VMEM((groups, rank, slots), BF)]
        + [pltpu.VMEM((rank, count), BF)] * 2 + [arrivals(1), arrivals(2), arrivals(4)])
    returned = exchange(remote, "group")
    own = call(own_scatter_kernel, "own_scatter", [(NEAR, (rank, rows), F32)],
               [(PLAIN, pull), (PLAIN, push), (NEAR, triplets)])
    rounded, partial = call(
        finish_kernel, "finish",
        [(NEAR, (rank, rows), BF), (NEAR, (rank, width), BF)],
        [(SCALAR, on), (NEAR, own), (NEAR, returned), (NEAR, wanted), (FAR, embeddings)],
        [pltpu.VMEM((rank, requests), BF), pltpu.VMEM((rows, width), BF), arrivals(1)])
    plane = exchange(partial.reshape(near, part, width), ("group", "dev"), level)
    plane = call(functools.partial(spread_kernel, factor=1.0), "plane",
                 [(NEAR, (levels, part, width), BF)], [(NEAR, plane)])
    whole = exchange(plane, "dev", column)
    whole = call(functools.partial(spread_kernel, factor=factor), "whole",
                 [(NEAR, (near, part, width), BF)], [(NEAR, whole)])
    whole = exchange(whole, ("group", "dev"), level)
    weight_grad = call(widen_kernel, "widen", [(PLAIN, (rank, width), F32)], [(NEAR, whole.reshape(rank, width))])
    row_grad = lax.dot_general(rounded, projection, (((0,), (0,)), ((), ())),
                               preferred_element_type=F32).astype(BF)
    return (row_grad, weight_grad)


def solution(mesh):
    return jax.shard_map(
        local,
        mesh=mesh,
        in_specs=(
            P(("group", "dev"), None),
            P(),
            P(None, ("group", "dev")),
            P(("group", "dev")),
            P(("group", "dev"), None),
        ),
        out_specs=(P(("group", "dev"), None), P()),
        check_vma=False,
    )
```

```python
import functools
import math

import jax
import jax.numpy as jnp
from jax import lax
from jax.experimental import pallas as pl
from jax.experimental.pallas import tpu as pltpu
from jax.sharding import PartitionSpec as P

distance_scale = 0.0625
margin = 1.0
pull_share = 0.5
BF = jnp.bfloat16
F32 = jnp.float32
BLOCK = 256
LANES = 128
STACK = 2
NT = (((1,), (1,)), ((), ()))
NN = (((1,), (0,)), ((), ()))
PARAMS = pltpu.CompilerParams(vmem_limit_bytes=24 * 1024 * 1024)


def row_numbers():
    return lax.broadcasted_iota(jnp.int32, (BLOCK, LANES), 0).astype(F32).astype(BF)


def hits(index, base, numbers):
    place = (index - base).astype(F32).astype(BF)
    return [
        jnp.broadcast_to(place[:, c : c + LANES], (BLOCK, LANES)) == numbers
        for c in range(0, index.shape[1], LANES)
    ]


def select(mask, value):
    return jnp.where(mask, jnp.full((BLOCK, LANES), value, BF), jnp.zeros((BLOCK, LANES), BF))


def one_hot(index, base, rows, numbers, value=1.0):
    blocks = []
    for r in range(0, rows, BLOCK):
        blocks.append(
            jnp.concatenate([select(m, value) for m in hits(index, base + r, numbers)], axis=1)
        )
    return blocks[0] if len(blocks) == 1 else jnp.concatenate(blocks, axis=0)


def dot(a, b, contract=NN):
    return lax.dot_general(a, b, contract, preferred_element_type=F32)


def project_kernel(embeddings_ref, projection_ref, out_ref, out_hbm, left):
    out_ref[...] = dot(projection_ref[...], embeddings_ref[...], NT).astype(BF)
    copy = pltpu.make_async_copy(out_ref, out_hbm, left.at[0])
    copy.start()
    copy.wait()


def serve_kernel(table_ref, wanted_ref, out_hbm, out_ref, left):
    numbers = row_numbers()
    groups, rank, slots = out_ref.shape
    step = groups // 4
    copies = []
    for i in range(4):
        first = i * step
        index = jnp.concatenate([wanted_ref[first + j] for j in range(step)], axis=1)
        served = dot(table_ref[...], one_hot(index, 0, table_ref.shape[1], numbers)).astype(BF)
        for j in range(step):
            out_ref[first + j] = served[:, j * slots : (j + 1) * slots]
        some = pl.ds(first, step)
        copies.append(pltpu.make_async_copy(out_ref.at[some], out_hbm.at[some], left.at[i]))
        copies[-1].start()
    for copy in copies:
        copy.wait()


def own_gather_kernel(table_ref, triplets_ref, anchor_ref, positive_ref, negative_hbm, negative_ref, left):
    numbers = row_numbers()
    rows = table_ref.shape[1]
    step = 512
    copy = pltpu.make_async_copy(negative_ref, negative_hbm, left.at[0])
    for row, out_ref in ((2, negative_ref), (0, anchor_ref), (1, positive_ref)):
        for i in range(0, triplets_ref.shape[1], step):
            at = pl.ds(i, step)
            out_ref[:, at] = dot(table_ref[...], one_hot(triplets_ref[row : row + 1, at], 0, rows, numbers)).astype(BF)
        if row == 2:
            copy.start()
    copy.wait()


def middle_kernel(fetched_ref, triplets_ref, cotangent_ref, anchor_ref, positive_ref, negative_hbm,
                  remote_hbm, pull_hbm, push_hbm,
                  table_ref, negative_ref, remote_ref, pull_ref, push_ref,
                  arrived, left, sent, *, own):
    numbers = row_numbers()
    groups, rank, slots = fetched_ref.shape
    rows = groups * slots
    count = triplets_ref.shape[1]
    parts = 4
    step = count // parts
    incoming = pltpu.make_async_copy(negative_hbm, negative_ref, arrived.at[0])
    incoming.start()
    outgoing = [pltpu.make_async_copy(pull_ref, pull_hbm, left.at[0]),
                pltpu.make_async_copy(push_ref, push_hbm, left.at[1])]
    for g in range(groups):
        table_ref[:, g * slots : (g + 1) * slots] = fetched_ref[g]
    for i in range(parts):
        at = pl.ds(i * step, step)
        positive = dot(table_ref[...], one_hot(triplets_ref[1:2, at], own, rows, numbers))
        negative = dot(table_ref[...], one_hot(triplets_ref[2:3, at], own, rows, numbers))
        if i == 0:
            incoming.wait()
        anchor = anchor_ref[:, at].astype(F32)
        to_positive = anchor - (positive_ref[:, at].astype(F32) + positive)
        to_negative = anchor - (negative_ref[:, at].astype(F32) + negative)
        near = distance_scale * jnp.sum(to_positive * to_positive, axis=0, keepdims=True)
        far = distance_scale * jnp.sum(to_negative * to_negative, axis=0, keepdims=True)
        gate = jax.nn.sigmoid(margin + near - far)
        weight = cotangent_ref[:, at]
        pull = 2.0 * distance_scale * weight * (1.0 - pull_share + pull_share * gate)
        push = 2.0 * distance_scale * weight * pull_share * gate
        pull_ref[:, at] = (-pull * to_positive).astype(BF)
        push_ref[:, at] = (push * to_negative).astype(BF)
    for copy in outgoing:
        copy.start()
    step = rows // parts
    per = step // slots
    for i in range(parts):
        base = own + i * step
        total = dot(pull_ref[...], one_hot(triplets_ref[1:2, :], base, step, numbers), NT)
        total = total + dot(push_ref[...], one_hot(triplets_ref[2:3, :], base, step, numbers), NT)
        total = total.astype(BF)
        for j in range(per):
            remote_ref[i * per + j] = total[:, j * slots : (j + 1) * slots]
        some = pl.ds(i * per, per)
        outgoing.append(pltpu.make_async_copy(remote_ref.at[some], remote_hbm.at[some], sent.at[i]))
        outgoing[-1].start()
    for copy in outgoing:
        copy.wait()


def own_scatter_kernel(pull_ref, push_ref, triplets_ref, out_ref):
    numbers = row_numbers()
    for base in range(0, out_ref.shape[1], BLOCK):
        anchor = hits(triplets_ref[0:1, :], base, numbers)
        parts = []
        for row in (1, 2):
            other = hits(triplets_ref[row : row + 1, :], base, numbers)
            parts.append(jnp.concatenate(
                [select(n, 1.0) - select(m, 1.0) for m, n in zip(anchor, other)], axis=1))
        out_ref[:, pl.ds(base, BLOCK)] = dot(pull_ref[...], parts[0], NT) + dot(push_ref[...], parts[1], NT)


def finish_kernel(on_ref, own_ref, returned_ref, wanted_ref, embeddings_hbm,
                  rounded_ref, partial_ref, back_ref, embeddings_ref, arrived):
    numbers = row_numbers()
    groups, rank, slots = returned_ref.shape
    copy = pltpu.make_async_copy(embeddings_hbm, embeddings_ref, arrived.at[0])
    copy.start()

    @pl.when(on_ref[0] >= 0)
    def _():
        for g in range(groups):
            back_ref[:, g * slots : (g + 1) * slots] = returned_ref[g]
        index = jnp.concatenate([wanted_ref[g] for g in range(groups)], axis=1)
        for base in range(0, own_ref.shape[1], BLOCK):
            at = pl.ds(base, BLOCK)
            total = dot(back_ref[...], one_hot(index, base, BLOCK, numbers), NT)
            rounded_ref[:, at] = (own_ref[:, at] + total).astype(BF)

    copy.wait()
    partial = dot(rounded_ref[...], embeddings_ref[...]).astype(BF)
    strip = partial_ref.shape[1]
    for i in range(partial_ref.shape[0] // rank):
        partial_ref[i * rank : (i + 1) * rank, :] = partial[:, i * strip : (i + 1) * strip]


def spread_kernel(parts_ref, out_ref, *, factor):
    total = parts_ref[0].astype(F32)
    for g in range(1, parts_ref.shape[0]):
        total = total + parts_ref[g].astype(F32)
    total = (total * factor).astype(out_ref.dtype)
    for g in range(out_ref.shape[0]):
        out_ref[g] = total


def widen_kernel(parts_ref, out_ref):
    rank = out_ref.shape[0]
    strip = parts_ref.shape[1]
    for i in range(parts_ref.shape[0] // rank):
        out_ref[:, i * strip : (i + 1) * strip] = parts_ref[i * rank : (i + 1) * rank, :].astype(F32)


NEAR, FAR, PLAIN, SCALAR = "near", "far", "plain", "scalar"
SPACES = {NEAR: pltpu.VMEM, FAR: pltpu.HBM, PLAIN: pltpu.HBM}
SPECS = {
    NEAR: pl.BlockSpec(memory_space=pltpu.VMEM),
    FAR: pl.BlockSpec(memory_space=pltpu.HBM),
    PLAIN: pl.BlockSpec(memory_space=pltpu.VMEM),
    SCALAR: pl.BlockSpec(memory_space=pltpu.SMEM),
}


def call(kernel, name, outs, ins, scratch=()):
    args = [a if place == SCALAR else pltpu.with_memory_space_constraint(a, SPACES[place]) for place, a in ins]
    shapes = [SPACES[place](dims, kind) for place, dims, kind in outs]
    result = pl.pallas_call(
        kernel, out_shape=shapes, in_specs=[SPECS[place] for place, _ in ins],
        out_specs=[SPECS[out[0]] for out in outs], scratch_shapes=scratch,
        compiler_params=PARAMS, name=name)(*args)
    return result if len(outs) > 1 else result[0]


def exchange(value, axis, groups=None):
    return lax.all_to_all(value, axis, split_axis=0, concat_axis=0, tiled=True, axis_index_groups=groups)


def local(embeddings, projection, triplets, cotangent, wanted_rows):
    rows, width = embeddings.shape
    rank = projection.shape[0]
    count = triplets.shape[1]
    groups, slots = wanted_rows.shape
    members = lax.axis_size("dev")
    cores = 2
    levels = members // cores
    stack = STACK
    near = groups * cores * stack
    part = rank // (groups * cores)
    strip = width // stack
    level = [
        [g * members + cores * (z * stack + b) + c for b in range(stack) for g in range(groups) for c in range(cores)]
        for z in range(levels // stack)]
    column = [
        [cores * (z * stack + b) + c for z in range(levels // stack)] for b in range(stack) for c in range(cores)]
    factor = 1.0 / math.sqrt(cotangent.shape[0] * groups * members)
    requests = groups * slots
    on = lax.axis_index("dev").astype(jnp.int32).reshape(1)

    def arrivals(n):
        return pltpu.SemaphoreType.DMA((n,))

    wanted = exchange(wanted_rows.reshape(groups, 1, slots), "group")
    table, table_hbm = call(project_kernel, "project", [(NEAR, (rank, rows), BF), (FAR, (rank, rows), BF)],
                            [(NEAR, embeddings), (NEAR, projection)], [arrivals(1)])
    served = call(serve_kernel, "serve", [(FAR, (groups, rank, slots), BF)], [(NEAR, table), (NEAR, wanted)],
                  [pltpu.VMEM((groups, rank, slots), BF), arrivals(4)])
    fetched = exchange(served, "group")
    anchor, positive, negative = call(
        own_gather_kernel, "own_gather",
        [(NEAR, (rank, count), BF), (NEAR, (rank, count), BF), (FAR, (rank, count), BF)],
        [(PLAIN, table_hbm), (NEAR, triplets)], [pltpu.VMEM((rank, count), BF), arrivals(1)])
    remote, pull, push = call(
        functools.partial(middle_kernel, own=rows), "middle",
        [(FAR, (groups, rank, slots), BF), (FAR, (rank, count), BF), (FAR, (rank, count), BF)],
        [(NEAR, fetched), (NEAR, triplets), (NEAR, cotangent.reshape(1, count)),
         (NEAR, anchor), (NEAR, positive), (FAR, negative)],
        [pltpu.VMEM((rank, requests), BF), pltpu.VMEM((rank, count), BF), pltpu.VMEM((groups, rank, slots), BF)]
        + [pltpu.VMEM((rank, count), BF)] * 2 + [arrivals(1), arrivals(2), arrivals(4)])
    returned = exchange(remote, "group")
    own = call(own_scatter_kernel, "own_scatter", [(NEAR, (rank, rows), F32)],
               [(PLAIN, pull), (PLAIN, push), (NEAR, triplets)])
    rounded, partial = call(
        finish_kernel, "finish",
        [(NEAR, (rank, rows), BF), (NEAR, (rank * stack, strip), BF)],
        [(SCALAR, on), (NEAR, own), (NEAR, returned), (NEAR, wanted), (FAR, embeddings)],
        [pltpu.VMEM((rank, requests), BF), pltpu.VMEM((rows, width), BF), arrivals(1)])
    plane = exchange(partial.reshape(near, part, strip), ("group", "dev"), level)
    plane = call(functools.partial(spread_kernel, factor=1.0), "plane",
                 [(NEAR, (levels // stack, part, strip), BF)], [(NEAR, plane)])
    whole = exchange(plane, "dev", column)
    whole = call(functools.partial(spread_kernel, factor=factor), "whole",
                 [(NEAR, (near, part, strip), BF)], [(NEAR, whole)])
    whole = exchange(whole, ("group", "dev"), level)
    weight_grad = call(widen_kernel, "widen", [(PLAIN, (rank, width), F32)], [(NEAR, whole.reshape(rank * stack, strip))])
    row_grad = lax.dot_general(rounded, projection, (((0,), (0,)), ((), ())),
                               preferred_element_type=F32).astype(BF)
    return (row_grad, weight_grad)


def solution(mesh):
    return jax.shard_map(
        local,
        mesh=mesh,
        in_specs=(
            P(("group", "dev"), None),
            P(),
            P(None, ("group", "dev")),
            P(("group", "dev")),
            P(("group", "dev"), None),
        ),
        out_specs=(P(("group", "dev"), None), P()),
        check_vma=False,
    )
```

```python
import functools
import math

import jax
import jax.numpy as jnp
from jax import lax
from jax.experimental import pallas as pl
from jax.experimental.pallas import tpu as pltpu
from jax.sharding import PartitionSpec as P

distance_scale = 0.0625
margin = 1.0
pull_share = 0.5
BF = jnp.bfloat16
F32 = jnp.float32
BLOCK = 256
LANES = 128
NT = (((1,), (1,)), ((), ()))
NN = (((1,), (0,)), ((), ()))
PARAMS = pltpu.CompilerParams(vmem_limit_bytes=24 * 1024 * 1024)


def row_numbers():
    return lax.broadcasted_iota(jnp.int32, (BLOCK, LANES), 0).astype(F32).astype(BF)


def hits(index, base, numbers):
    place = (index - base).astype(F32).astype(BF)
    return [
        jnp.broadcast_to(place[:, c : c + LANES], (BLOCK, LANES)) == numbers
        for c in range(0, index.shape[1], LANES)
    ]


def select(mask, value):
    return jnp.where(mask, jnp.full((BLOCK, LANES), value, BF), jnp.zeros((BLOCK, LANES), BF))


def one_hot(index, base, rows, numbers, value=1.0):
    blocks = []
    for r in range(0, rows, BLOCK):
        blocks.append(
            jnp.concatenate([select(m, value) for m in hits(index, base + r, numbers)], axis=1)
        )
    return blocks[0] if len(blocks) == 1 else jnp.concatenate(blocks, axis=0)


def dot(a, b, contract=NN):
    return lax.dot_general(a, b, contract, preferred_element_type=F32)


def project_kernel(embeddings_ref, projection_ref, out_ref, out_hbm, left):
    out_ref[...] = dot(projection_ref[...], embeddings_ref[...], NT).astype(BF)
    copy = pltpu.make_async_copy(out_ref, out_hbm, left.at[0])
    copy.start()
    copy.wait()


def serve_kernel(table_ref, wanted_ref, out_hbm, out_ref, left):
    numbers = row_numbers()
    groups, rank, slots = out_ref.shape
    step = groups // 4
    copies = []
    for i in range(4):
        first = i * step
        index = jnp.concatenate([wanted_ref[first + j] for j in range(step)], axis=1)
        served = dot(table_ref[...], one_hot(index, 0, table_ref.shape[1], numbers)).astype(BF)
        for j in range(step):
            out_ref[first + j] = served[:, j * slots : (j + 1) * slots]
        some = pl.ds(first, step)
        copies.append(pltpu.make_async_copy(out_ref.at[some], out_hbm.at[some], left.at[i]))
        copies[-1].start()
    for copy in copies:
        copy.wait()


def own_gather_kernel(table_ref, triplets_ref, anchor_ref, positive_ref, negative_hbm, negative_ref, left):
    numbers = row_numbers()
    rows = table_ref.shape[1]
    step = 512
    copy = pltpu.make_async_copy(negative_ref, negative_hbm, left.at[0])
    for row, out_ref in ((2, negative_ref), (0, anchor_ref), (1, positive_ref)):
        for i in range(0, triplets_ref.shape[1], step):
            at = pl.ds(i, step)
            out_ref[:, at] = dot(table_ref[...], one_hot(triplets_ref[row : row + 1, at], 0, rows, numbers)).astype(BF)
        if row == 2:
            copy.start()
    copy.wait()


def middle_kernel(fetched_ref, triplets_ref, cotangent_ref, anchor_ref, positive_ref, negative_hbm,
                  remote_hbm, pull_hbm, push_hbm,
                  table_ref, negative_ref, remote_ref, pull_ref, push_ref,
                  arrived, left, sent, *, own):
    numbers = row_numbers()
    groups, rank, slots = fetched_ref.shape
    rows = groups * slots
    count = triplets_ref.shape[1]
    parts = 4
    step = count // parts
    incoming = pltpu.make_async_copy(negative_hbm, negative_ref, arrived.at[0])
    incoming.start()
    outgoing = [pltpu.make_async_copy(pull_ref, pull_hbm, left.at[0]),
                pltpu.make_async_copy(push_ref, push_hbm, left.at[1])]
    for g in range(groups):
        table_ref[:, g * slots : (g + 1) * slots] = fetched_ref[g]
    for i in range(parts):
        at = pl.ds(i * step, step)
        positive = dot(table_ref[...], one_hot(triplets_ref[1:2, at], own, rows, numbers))
        negative = dot(table_ref[...], one_hot(triplets_ref[2:3, at], own, rows, numbers))
        if i == 0:
            incoming.wait()
        anchor = anchor_ref[:, at].astype(F32)
        to_positive = anchor - (positive_ref[:, at].astype(F32) + positive)
        to_negative = anchor - (negative_ref[:, at].astype(F32) + negative)
        near = distance_scale * jnp.sum(to_positive * to_positive, axis=0, keepdims=True)
        far = distance_scale * jnp.sum(to_negative * to_negative, axis=0, keepdims=True)
        gate = jax.nn.sigmoid(margin + near - far)
        weight = cotangent_ref[:, at]
        pull = 2.0 * distance_scale * weight * (1.0 - pull_share + pull_share * gate)
        push = 2.0 * distance_scale * weight * pull_share * gate
        pull_ref[:, at] = (-pull * to_positive).astype(BF)
        push_ref[:, at] = (push * to_negative).astype(BF)
    for copy in outgoing:
        copy.start()
    step = rows // parts
    per = step // slots
    for i in range(parts):
        base = own + i * step
        total = dot(pull_ref[...], one_hot(triplets_ref[1:2, :], base, step, numbers), NT)
        total = total + dot(push_ref[...], one_hot(triplets_ref[2:3, :], base, step, numbers), NT)
        total = total.astype(BF)
        for j in range(per):
            remote_ref[i * per + j] = total[:, j * slots : (j + 1) * slots]
        some = pl.ds(i * per, per)
        outgoing.append(pltpu.make_async_copy(remote_ref.at[some], remote_hbm.at[some], sent.at[i]))
        outgoing[-1].start()
    for copy in outgoing:
        copy.wait()


def own_scatter_kernel(pull_ref, push_ref, triplets_ref, out_ref):
    numbers = row_numbers()
    for base in range(0, out_ref.shape[1], BLOCK):
        anchor = hits(triplets_ref[0:1, :], base, numbers)
        parts = []
        for row in (1, 2):
            other = hits(triplets_ref[row : row + 1, :], base, numbers)
            parts.append(jnp.concatenate(
                [select(n, 1.0) - select(m, 1.0) for m, n in zip(anchor, other)], axis=1))
        out_ref[:, pl.ds(base, BLOCK)] = dot(pull_ref[...], parts[0], NT) + dot(push_ref[...], parts[1], NT)


def finish_kernel(on_ref, own_ref, returned_ref, wanted_ref, embeddings_hbm,
                  rounded_ref, partial_hbm, back_ref, embeddings_ref, partial_ref, arrived, left):
    numbers = row_numbers()
    groups, rank, slots = returned_ref.shape
    copy = pltpu.make_async_copy(embeddings_hbm, embeddings_ref, arrived.at[0])
    copy.start()

    @pl.when(on_ref[0] >= 0)
    def _():
        for g in range(groups):
            back_ref[:, g * slots : (g + 1) * slots] = returned_ref[g]
        index = jnp.concatenate([wanted_ref[g] for g in range(groups)], axis=1)
        for base in range(0, own_ref.shape[1], BLOCK):
            at = pl.ds(base, BLOCK)
            total = dot(back_ref[...], one_hot(index, base, BLOCK, numbers), NT)
            rounded_ref[:, at] = (own_ref[:, at] + total).astype(BF)

    copy.wait()
    outgoing = []
    half = rank // 2
    for i in range(2):
        at = pl.ds(i * half, half)
        partial_ref[at, :] = dot(rounded_ref[at, :], embeddings_ref[...]).astype(BF)
        outgoing.append(pltpu.make_async_copy(partial_ref.at[at], partial_hbm.at[at], left.at[i]))
        outgoing[-1].start()
    for copy in outgoing:
        copy.wait()


def spread_kernel(parts_ref, out_ref, *, factor):
    total = parts_ref[0].astype(F32)
    for g in range(1, parts_ref.shape[0]):
        total = total + parts_ref[g].astype(F32)
    total = (total * factor).astype(out_ref.dtype)
    for g in range(out_ref.shape[0]):
        out_ref[g] = total


def widen_kernel(parts_ref, out_ref):
    out_ref[...] = parts_ref[...].astype(F32)


NEAR, FAR, PLAIN, SCALAR = "near", "far", "plain", "scalar"
SPACES = {NEAR: pltpu.VMEM, FAR: pltpu.HBM, PLAIN: pltpu.HBM}
SPECS = {
    NEAR: pl.BlockSpec(memory_space=pltpu.VMEM),
    FAR: pl.BlockSpec(memory_space=pltpu.HBM),
    PLAIN: pl.BlockSpec(memory_space=pltpu.VMEM),
    SCALAR: pl.BlockSpec(memory_space=pltpu.SMEM),
}


def call(kernel, name, outs, ins, scratch=()):
    args = [a if place == SCALAR else pltpu.with_memory_space_constraint(a, SPACES[place]) for place, a in ins]
    shapes = [SPACES[place](dims, kind) for place, dims, kind in outs]
    result = pl.pallas_call(
        kernel, out_shape=shapes, in_specs=[SPECS[place] for place, _ in ins],
        out_specs=[SPECS[out[0]] for out in outs], scratch_shapes=scratch,
        compiler_params=PARAMS, name=name)(*args)
    return result if len(outs) > 1 else result[0]


def exchange(value, axis, groups=None):
    return lax.all_to_all(value, axis, split_axis=0, concat_axis=0, tiled=True, axis_index_groups=groups)


def local(embeddings, projection, triplets, cotangent, wanted_rows):
    rows, width = embeddings.shape
    rank = projection.shape[0]
    count = triplets.shape[1]
    groups, slots = wanted_rows.shape
    members = lax.axis_size("dev")
    cores = 2
    levels = members // cores
    near = groups * cores
    part = rank // near
    level = [[g * members + cores * z + c for g in range(groups) for c in range(cores)] for z in range(levels)]
    column = [[cores * z + c for z in range(levels)] for c in range(cores)]
    factor = 1.0 / math.sqrt(cotangent.shape[0] * groups * members)
    requests = groups * slots
    on = lax.axis_index("dev").astype(jnp.int32).reshape(1)

    def arrivals(n):
        return pltpu.SemaphoreType.DMA((n,))

    wanted = exchange(wanted_rows.reshape(groups, 1, slots), "group")
    table, table_hbm = call(project_kernel, "project", [(NEAR, (rank, rows), BF), (FAR, (rank, rows), BF)],
                            [(NEAR, embeddings), (NEAR, projection)], [arrivals(1)])
    served = call(serve_kernel, "serve", [(FAR, (groups, rank, slots), BF)], [(NEAR, table), (NEAR, wanted)],
                  [pltpu.VMEM((groups, rank, slots), BF), arrivals(4)])
    fetched = exchange(served, "group")
    anchor, positive, negative = call(
        own_gather_kernel, "own_gather",
        [(NEAR, (rank, count), BF), (NEAR, (rank, count), BF), (FAR, (rank, count), BF)],
        [(PLAIN, table_hbm), (NEAR, triplets)], [pltpu.VMEM((rank, count), BF), arrivals(1)])
    remote, pull, push = call(
        functools.partial(middle_kernel, own=rows), "middle",
        [(FAR, (groups, rank, slots), BF), (FAR, (rank, count), BF), (FAR, (rank, count), BF)],
        [(NEAR, fetched), (NEAR, triplets), (NEAR, cotangent.reshape(1, count)),
         (NEAR, anchor), (NEAR, positive), (FAR, negative)],
        [pltpu.VMEM((rank, requests), BF), pltpu.VMEM((rank, count), BF), pltpu.VMEM((groups, rank, slots), BF)]
        + [pltpu.VMEM((rank, count), BF)] * 2 + [arrivals(1), arrivals(2), arrivals(4)])
    returned = exchange(remote, "group")
    own = call(own_scatter_kernel, "own_scatter", [(NEAR, (rank, rows), F32)],
               [(PLAIN, pull), (PLAIN, push), (NEAR, triplets)])
    rounded, partial = call(
        finish_kernel, "finish",
        [(NEAR, (rank, rows), BF), (FAR, (rank, width), BF)],
        [(SCALAR, on), (NEAR, own), (NEAR, returned), (NEAR, wanted), (FAR, embeddings)],
        [pltpu.VMEM((rank, requests), BF), pltpu.VMEM((rows, width), BF), pltpu.VMEM((rank, width), BF),
         arrivals(1), arrivals(2)])
    plane = exchange(partial.reshape(near, part, width), ("group", "dev"), level)
    row_grad = lax.dot_general(rounded, projection, (((0,), (0,)), ((), ())),
                               preferred_element_type=F32).astype(BF)
    plane, row_grad = lax.optimization_barrier((plane, row_grad))
    plane = call(functools.partial(spread_kernel, factor=1.0), "plane",
                 [(NEAR, (levels, part, width), BF)], [(NEAR, plane)])
    whole = exchange(plane, "dev", column)
    whole = call(functools.partial(spread_kernel, factor=factor), "whole",
                 [(NEAR, (near, part, width), BF)], [(NEAR, whole)])
    whole = exchange(whole, ("group", "dev"), level)
    weight_grad = call(widen_kernel, "widen", [(PLAIN, (rank, width), F32)], [(NEAR, whole.reshape(rank, width))])
    return (row_grad, weight_grad)


def solution(mesh):
    return jax.shard_map(
        local,
        mesh=mesh,
        in_specs=(
            P(("group", "dev"), None),
            P(),
            P(None, ("group", "dev")),
            P(("group", "dev")),
            P(("group", "dev"), None),
        ),
        out_specs=(P(("group", "dev"), None), P()),
        check_vma=False,
    )
```

```python
import functools
import math

import jax
import jax.numpy as jnp
from jax import lax
from jax.experimental import pallas as pl
from jax.experimental.pallas import tpu as pltpu
from jax.sharding import PartitionSpec as P

distance_scale = 0.0625
margin = 1.0
pull_share = 0.5
BF = jnp.bfloat16
F32 = jnp.float32
BLOCK = 256
LANES = 128
STACK = 2
NT = (((1,), (1,)), ((), ()))
NN = (((1,), (0,)), ((), ()))
PARAMS = pltpu.CompilerParams(vmem_limit_bytes=24 * 1024 * 1024)


def row_numbers():
    return lax.broadcasted_iota(jnp.int32, (BLOCK, LANES), 0).astype(F32).astype(BF)


def hits(index, base, numbers):
    place = (index - base).astype(F32).astype(BF)
    return [
        jnp.broadcast_to(place[:, c : c + LANES], (BLOCK, LANES)) == numbers
        for c in range(0, index.shape[1], LANES)
    ]


def select(mask, value):
    return jnp.where(mask, jnp.full((BLOCK, LANES), value, BF), jnp.zeros((BLOCK, LANES), BF))


def one_hot(index, base, rows, numbers, value=1.0):
    blocks = []
    for r in range(0, rows, BLOCK):
        blocks.append(
            jnp.concatenate([select(m, value) for m in hits(index, base + r, numbers)], axis=1)
        )
    return blocks[0] if len(blocks) == 1 else jnp.concatenate(blocks, axis=0)


def dot(a, b, contract=NN):
    return lax.dot_general(a, b, contract, preferred_element_type=F32)


def project_kernel(embeddings_ref, projection_ref, out_ref, out_hbm, left):
    out_ref[...] = dot(projection_ref[...], embeddings_ref[...], NT).astype(BF)
    copy = pltpu.make_async_copy(out_ref, out_hbm, left.at[0])
    copy.start()
    copy.wait()


def serve_kernel(table_ref, wanted_ref, out_hbm, out_ref, left):
    numbers = row_numbers()
    groups, rank, slots = out_ref.shape
    step = groups // 4
    copies = []
    for i in range(4):
        first = i * step
        index = jnp.concatenate([wanted_ref[first + j] for j in range(step)], axis=1)
        served = dot(table_ref[...], one_hot(index, 0, table_ref.shape[1], numbers)).astype(BF)
        for j in range(step):
            out_ref[first + j] = served[:, j * slots : (j + 1) * slots]
        some = pl.ds(first, step)
        copies.append(pltpu.make_async_copy(out_ref.at[some], out_hbm.at[some], left.at[i]))
        copies[-1].start()
    for copy in copies:
        copy.wait()


def own_gather_kernel(table_ref, triplets_ref, anchor_ref, positive_ref, negative_hbm, negative_ref, left):
    numbers = row_numbers()
    rows = table_ref.shape[1]
    step = 512
    copy = pltpu.make_async_copy(negative_ref, negative_hbm, left.at[0])
    for row, out_ref in ((2, negative_ref), (0, anchor_ref), (1, positive_ref)):
        for i in range(0, triplets_ref.shape[1], step):
            at = pl.ds(i, step)
            out_ref[:, at] = dot(table_ref[...], one_hot(triplets_ref[row : row + 1, at], 0, rows, numbers)).astype(BF)
        if row == 2:
            copy.start()
    copy.wait()


def middle_kernel(fetched_ref, triplets_ref, cotangent_ref, anchor_ref, positive_ref, negative_hbm,
                  remote_hbm, pull_hbm, push_hbm,
                  table_ref, negative_ref, remote_ref, pull_ref, push_ref,
                  arrived, left, sent, *, own):
    numbers = row_numbers()
    groups, rank, slots = fetched_ref.shape
    rows = groups * slots
    count = triplets_ref.shape[1]
    parts = 4
    step = count // parts
    incoming = pltpu.make_async_copy(negative_hbm, negative_ref, arrived.at[0])
    incoming.start()
    outgoing = [pltpu.make_async_copy(pull_ref, pull_hbm, left.at[0]),
                pltpu.make_async_copy(push_ref, push_hbm, left.at[1])]
    for g in range(groups):
        table_ref[:, g * slots : (g + 1) * slots] = fetched_ref[g]
    for i in range(parts):
        at = pl.ds(i * step, step)
        positive = dot(table_ref[...], one_hot(triplets_ref[1:2, at], own, rows, numbers))
        negative = dot(table_ref[...], one_hot(triplets_ref[2:3, at], own, rows, numbers))
        if i == 0:
            incoming.wait()
        anchor = anchor_ref[:, at].astype(F32)
        to_positive = anchor - (positive_ref[:, at].astype(F32) + positive)
        to_negative = anchor - (negative_ref[:, at].astype(F32) + negative)
        near = distance_scale * jnp.sum(to_positive * to_positive, axis=0, keepdims=True)
        far = distance_scale * jnp.sum(to_negative * to_negative, axis=0, keepdims=True)
        gate = jax.nn.sigmoid(margin + near - far)
        weight = cotangent_ref[:, at]
        pull = 2.0 * distance_scale * weight * (1.0 - pull_share + pull_share * gate)
        push = 2.0 * distance_scale * weight * pull_share * gate
        pull_ref[:, at] = (-pull * to_positive).astype(BF)
        push_ref[:, at] = (push * to_negative).astype(BF)
    for copy in outgoing:
        copy.start()
    step = rows // parts
    per = step // slots
    for i in range(parts):
        base = own + i * step
        total = dot(pull_ref[...], one_hot(triplets_ref[1:2, :], base, step, numbers), NT)
        total = total + dot(push_ref[...], one_hot(triplets_ref[2:3, :], base, step, numbers), NT)
        total = total.astype(BF)
        for j in range(per):
            remote_ref[i * per + j] = total[:, j * slots : (j + 1) * slots]
        some = pl.ds(i * per, per)
        outgoing.append(pltpu.make_async_copy(remote_ref.at[some], remote_hbm.at[some], sent.at[i]))
        outgoing[-1].start()
    for copy in outgoing:
        copy.wait()


def own_scatter_kernel(pull_ref, push_ref, triplets_ref, out_ref):
    numbers = row_numbers()
    for base in range(0, out_ref.shape[1], BLOCK):
        anchor = hits(triplets_ref[0:1, :], base, numbers)
        parts = []
        for row in (1, 2):
            other = hits(triplets_ref[row : row + 1, :], base, numbers)
            parts.append(jnp.concatenate(
                [select(n, 1.0) - select(m, 1.0) for m, n in zip(anchor, other)], axis=1))
        out_ref[:, pl.ds(base, BLOCK)] = dot(pull_ref[...], parts[0], NT) + dot(push_ref[...], parts[1], NT)


def finish_kernel(on_ref, own_ref, returned_ref, wanted_ref, embeddings_hbm,
                  rounded_ref, partial_hbm, back_ref, embeddings_ref, partial_ref, arrived, left):
    numbers = row_numbers()
    groups, rank, slots = returned_ref.shape
    copy = pltpu.make_async_copy(embeddings_hbm, embeddings_ref, arrived.at[0])
    copy.start()

    @pl.when(on_ref[0] >= 0)
    def _():
        for g in range(groups):
            back_ref[:, g * slots : (g + 1) * slots] = returned_ref[g]
        index = jnp.concatenate([wanted_ref[g] for g in range(groups)], axis=1)
        for base in range(0, own_ref.shape[1], BLOCK):
            at = pl.ds(base, BLOCK)
            total = dot(back_ref[...], one_hot(index, base, BLOCK, numbers), NT)
            rounded_ref[:, at] = (own_ref[:, at] + total).astype(BF)

    copy.wait()
    outgoing = []
    strip = partial_ref.shape[1]
    for i in range(partial_ref.shape[0] // rank):
        at = pl.ds(i * rank, rank)
        partial_ref[at, :] = dot(rounded_ref[...], embeddings_ref[:, i * strip : (i + 1) * strip]).astype(BF)
        outgoing.append(pltpu.make_async_copy(partial_ref.at[at], partial_hbm.at[at], left.at[i]))
        outgoing[-1].start()
    for copy in outgoing:
        copy.wait()


def spread_kernel(parts_ref, out_ref, *, factor):
    total = parts_ref[0].astype(F32)
    for g in range(1, parts_ref.shape[0]):
        total = total + parts_ref[g].astype(F32)
    total = (total * factor).astype(out_ref.dtype)
    for g in range(out_ref.shape[0]):
        out_ref[g] = total


def widen_kernel(parts_ref, out_ref):
    rank = out_ref.shape[0]
    strip = parts_ref.shape[1]
    for i in range(parts_ref.shape[0] // rank):
        out_ref[:, i * strip : (i + 1) * strip] = parts_ref[i * rank : (i + 1) * rank, :].astype(F32)


NEAR, FAR, PLAIN, SCALAR = "near", "far", "plain", "scalar"
SPACES = {NEAR: pltpu.VMEM, FAR: pltpu.HBM, PLAIN: pltpu.HBM}
SPECS = {
    NEAR: pl.BlockSpec(memory_space=pltpu.VMEM),
    FAR: pl.BlockSpec(memory_space=pltpu.HBM),
    PLAIN: pl.BlockSpec(memory_space=pltpu.VMEM),
    SCALAR: pl.BlockSpec(memory_space=pltpu.SMEM),
}


def call(kernel, name, outs, ins, scratch=()):
    args = [a if place == SCALAR else pltpu.with_memory_space_constraint(a, SPACES[place]) for place, a in ins]
    shapes = [SPACES[place](dims, kind) for place, dims, kind in outs]
    result = pl.pallas_call(
        kernel, out_shape=shapes, in_specs=[SPECS[place] for place, _ in ins],
        out_specs=[SPECS[out[0]] for out in outs], scratch_shapes=scratch,
        compiler_params=PARAMS, name=name)(*args)
    return result if len(outs) > 1 else result[0]


def exchange(value, axis, groups=None):
    return lax.all_to_all(value, axis, split_axis=0, concat_axis=0, tiled=True, axis_index_groups=groups)


def local(embeddings, projection, triplets, cotangent, wanted_rows):
    rows, width = embeddings.shape
    rank = projection.shape[0]
    count = triplets.shape[1]
    groups, slots = wanted_rows.shape
    members = lax.axis_size("dev")
    cores = 2
    levels = members // cores
    stack = STACK
    near = groups * cores * stack
    part = rank // (groups * cores)
    strip = width // stack
    level = [
        [g * members + cores * (z * stack + b) + c for b in range(stack) for g in range(groups) for c in range(cores)]
        for z in range(levels // stack)]
    column = [
        [cores * (z * stack + b) + c for z in range(levels // stack)] for b in range(stack) for c in range(cores)]
    factor = 1.0 / math.sqrt(cotangent.shape[0] * groups * members)
    requests = groups * slots
    on = lax.axis_index("dev").astype(jnp.int32).reshape(1)

    def arrivals(n):
        return pltpu.SemaphoreType.DMA((n,))

    wanted = exchange(wanted_rows.reshape(groups, 1, slots), "group")
    table, table_hbm = call(project_kernel, "project", [(NEAR, (rank, rows), BF), (FAR, (rank, rows), BF)],
                            [(NEAR, embeddings), (NEAR, projection)], [arrivals(1)])
    served = call(serve_kernel, "serve", [(FAR, (groups, rank, slots), BF)], [(NEAR, table), (NEAR, wanted)],
                  [pltpu.VMEM((groups, rank, slots), BF), arrivals(4)])
    fetched = exchange(served, "group")
    anchor, positive, negative = call(
        own_gather_kernel, "own_gather",
        [(NEAR, (rank, count), BF), (NEAR, (rank, count), BF), (FAR, (rank, count), BF)],
        [(PLAIN, table_hbm), (NEAR, triplets)], [pltpu.VMEM((rank, count), BF), arrivals(1)])
    remote, pull, push = call(
        functools.partial(middle_kernel, own=rows), "middle",
        [(FAR, (groups, rank, slots), BF), (FAR, (rank, count), BF), (FAR, (rank, count), BF)],
        [(NEAR, fetched), (NEAR, triplets), (NEAR, cotangent.reshape(1, count)),
         (NEAR, anchor), (NEAR, positive), (FAR, negative)],
        [pltpu.VMEM((rank, requests), BF), pltpu.VMEM((rank, count), BF), pltpu.VMEM((groups, rank, slots), BF)]
        + [pltpu.VMEM((rank, count), BF)] * 2 + [arrivals(1), arrivals(2), arrivals(4)])
    returned = exchange(remote, "group")
    own = call(own_scatter_kernel, "own_scatter", [(NEAR, (rank, rows), F32)],
               [(PLAIN, pull), (PLAIN, push), (NEAR, triplets)])
    rounded, partial = call(
        finish_kernel, "finish",
        [(NEAR, (rank, rows), BF), (FAR, (rank * stack, strip), BF)],
        [(SCALAR, on), (NEAR, own), (NEAR, returned), (NEAR, wanted), (FAR, embeddings)],
        [pltpu.VMEM((rank, requests), BF), pltpu.VMEM((rows, width), BF), pltpu.VMEM((rank * stack, strip), BF),
         arrivals(1), arrivals(2)])
    plane = exchange(partial.reshape(near, part, strip), ("group", "dev"), level)
    row_grad = lax.dot_general(rounded, projection, (((0,), (0,)), ((), ())),
                               preferred_element_type=F32).astype(BF)
    plane, row_grad = lax.optimization_barrier((plane, row_grad))
    plane = call(functools.partial(spread_kernel, factor=1.0), "plane",
                 [(NEAR, (levels // stack, part, strip), BF)], [(NEAR, plane)])
    whole = exchange(plane, "dev", column)
    whole = call(functools.partial(spread_kernel, factor=factor), "whole",
                 [(NEAR, (near, part, strip), BF)], [(NEAR, whole)])
    whole = exchange(whole, ("group", "dev"), level)
    weight_grad = call(widen_kernel, "widen", [(PLAIN, (rank, width), F32)], [(NEAR, whole.reshape(rank * stack, strip))])
    return (row_grad, weight_grad)


def solution(mesh):
    return jax.shard_map(
        local,
        mesh=mesh,
        in_specs=(
            P(("group", "dev"), None),
            P(),
            P(None, ("group", "dev")),
            P(("group", "dev")),
            P(("group", "dev"), None),
        ),
        out_specs=(P(("group", "dev"), None), P()),
        check_vma=False,
    )
```
